32 devices in a mesh: groups: 2 (over y), expert: 8 (over z, x), dp: 2 (over core).
Axes of the slice: x: 2, y: 2, z: 4, core: 2. Of those that a mesh axis runs over, the one named last changes fastest.
Arguments:
- tokens: bfloat16 [4096, 3584], P(('groups', 'expert', 'dp')), parts along dimension 0, may hold values from -6 to 6
- grad_out: bfloat16 [4096, 3584], P(('groups', 'expert', 'dp')), parts along dimension 0, may hold values from -6 to 6
- routing: int32 [4096, 8], P(('groups', 'expert', 'dp')), parts along dimension 0, may hold values from 0 to 63, as said below
- gates: float32 [4096, 8], P(('groups', 'expert', 'dp')), parts along dimension 0, may hold values from 0.05 to 0.5
- modality: int32 [4096], P(('groups', 'expert', 'dp')), parts along dimension 0, may hold values from 0 to 1, as said below
- hot_experts: int32 [4], P('groups'), parts along dimension 0, may hold values from 0 to 7, as said below
- gate_weight: bfloat16 [16384, 3584], P('expert'), may hold values from -0.09375 to 0.09375
- up_weight: bfloat16 [16384, 3584], P('expert'), may hold values from -0.09375 to 0.09375
- down_weight: bfloat16 [16384, 3584], P('expert'), may hold values from -0.125 to 0.125
Outputs:
- grad_tokens: bfloat16 [4096, 3584], P(('groups', 'expert', 'dp')), parts along dimension 0
- grad_gate: bfloat16 [32768, 3584], P(('groups', 'expert', 'dp')), parts along dimension 0
- grad_up: bfloat16 [32768, 3584], P(('groups', 'expert', 'dp')), parts along dimension 0
- grad_down: bfloat16 [32768, 3584], P(('groups', 'expert', 'dp')), parts along dimension 0
The draws below stay inside these ranges and needn't reach their ends.
There are 2 independent parts, one for each index of `groups`. The reference program is written for one: setup_inputs(seed, part) draws one part's arguments, and reference() takes and returns one part's arrays. A program takes and returns all parts, laid end to end along the dimension named above; an argument that names none is the same for every part. Nothing has to cross between parts.
Inputs may be any that keep to these rules, and one draw needn't show every extreme that they name: `routing`: each token names 8 different experts. Among the 128 tokens of each device, every expert in flight that is not hot is named by exactly 2 text tokens, a text token names at most one expert in flight, an image token names none in flight outside its last 2 entries, and no text token names a hot expert. `modality`: exactly 8 image tokens among the 128 tokens of each device. `hot_experts`: 2 different experts in flight.
All inputs are finite; a program needn't handle non-finite values.
Results may differ from the reference program's by a relative error of at most 0.0061.
Values may be sent and summed in bfloat16 or wider, within the bound.
No kernel may reach another device: no remote copies, remote signals or barrier semaphores. Data moves between devices by JAX's collectives and lax.ppermute only.
A program may use at most 384 MiB of HBM per device.

```python
import math
import jax
import jax.numpy as jnp
from jax import lax

D = 3584
FF = 2048
EXPERTS = 64
TOPK = 8
FLIGHT = 8
NHOT = 2
TOK_DEV = 128
HOTCAP = 8
COLD = 2
SPLIT = 1
HD = 2048
TOKENS = 2048


def layout_draw(key):
    blocks_count = TOKENS // TOK_DEV
    key_hot = jax.random.fold_in(key, 101)
    key_role = jax.random.fold_in(key, 102)
    key_other = jax.random.fold_in(key, 103)
    key_column = jax.random.fold_in(key, 104)
    order = jax.random.permutation(key_hot, FLIGHT).astype(jnp.int32)
    hot_list = order[:NHOT]
    cold_list = order[NHOT:]
    role_keys = jax.random.split(key_role, blocks_count)
    roles = jax.vmap(lambda sub_key: jax.random.permutation(sub_key, TOK_DEV))(role_keys)
    roles = roles.reshape(TOKENS).astype(jnp.int32)
    image = roles < HOTCAP
    cold_slot = roles - HOTCAP
    has_cold = (cold_slot >= 0) & (cold_slot < COLD * (FLIGHT - NHOT))
    cold_index = jnp.clip(cold_slot // COLD, 0, FLIGHT - NHOT - 1)
    cold_id = cold_list[cold_index]
    other_keys = jax.random.split(key_other, TOKENS)
    outside = jax.vmap(lambda sub_key: jax.random.permutation(sub_key, EXPERTS - FLIGHT)[:TOPK])(other_keys)
    base = (outside + FLIGHT).astype(jnp.int32)
    column = jax.random.randint(key_column, (TOKENS,), 0, TOPK)
    position = jnp.arange(TOPK, dtype=jnp.int32)[None, :]
    routing = jnp.where(has_cold[:, None] & (position == column[:, None]), cold_id[:, None], base)
    return (hot_list, routing.astype(jnp.int32), image.astype(jnp.int32))


def draw_routing(key, part):
    return layout_draw(key)[1]


def draw_modality(key, part):
    return layout_draw(key)[2]


def draw_hot_experts(key, part):
    return layout_draw(key)[0]


def steps_of(stream_key, shape, pieces, least, largest):
    def one(dim, parts):
        steps = jax.random.uniform(jax.random.fold_in(jax.random.fold_in(stream_key, 6), dim), (parts,), jnp.float32, least / len(pieces), largest / len(pieces))
        return jnp.repeat(jnp.exp(steps), shape[dim] // parts).reshape((-1,) + (1,) * (len(shape) - dim - 1))

    level = one(*pieces[0])
    for cut in pieces[1:]:
        level = level * one(*cut)
    return level


def normal_values(key, extent, spread, most, pieces=(), held_as=jnp.bfloat16):
    values = jax.random.normal(key, extent, jnp.float32) * spread
    if len(pieces) > 0:
        values = steps_of(key, extent, pieces, -0.22, 0.18) * values
    return jnp.clip(values, min=-most, max=most).astype(held_as)


def setup_inputs(seed: int = 0, part: int = 0) -> dict:
    key_list = jax.random.split(jax.random.key(seed), 10)
    part_splits = jax.random.split(jax.random.fold_in(key_list[9], part), 10)
    return {
        "tokens": normal_values(part_splits[0], (TOKENS, D), 1.0, 6.0, ((0, 16),)),
        "grad_out": normal_values(part_splits[1], (TOKENS, D), 1.0, 6.0, ((0, 16),)),
        "routing": draw_routing(jax.random.fold_in(jax.random.fold_in(key_list[9], part), 71), part),
        "gates": jnp.clip(jnp.exp(math.log(0.5) - 2.3025851 * jax.random.uniform(part_splits[3], (TOKENS, TOPK), jnp.float32) ** steps_of(part_splits[3], (TOKENS, TOPK), ((0, 16),), -0.2, 0.2)), 0.05, 0.5),
        "modality": draw_modality(jax.random.fold_in(jax.random.fold_in(key_list[9], part), 71), part),
        "hot_experts": draw_hot_experts(jax.random.fold_in(jax.random.fold_in(key_list[9], part), 71), part),
        "gate_weight": normal_values(key_list[6], (FLIGHT * FF, D), D ** -0.5, 0.09375, ((0, 8),)),
        "up_weight": normal_values(key_list[7], (FLIGHT * FF, D), D ** -0.5, 0.09375, ((0, 8),)),
        "down_weight": normal_values(key_list[8], (FLIGHT * FF, D), FF ** -0.5, 0.125, ((0, 8),)),
    }


def reference(tokens, grad_out, routing, gates, modality, hot_experts, gate_weight, up_weight, down_weight):
    position = lax.broadcasted_iota(jnp.int32, (TOKENS, TOPK), 1)
    pinned_slot = position - (TOPK - NHOT)
    pick_table = pinned_slot[:, :, None] == jnp.arange(NHOT, dtype=jnp.int32)[None, None, :]
    hot_pick = jnp.sum(jnp.where(pick_table, hot_experts[None, None, :], 0), axis=2).astype(jnp.int32)
    chosen = jnp.where((modality[:, None] == 1) & (pinned_slot >= 0), hot_pick, routing)
    matches = chosen[:, :, None] == jnp.arange(FLIGHT, dtype=jnp.int32)[None, None, :]
    expert_gate = jnp.sum(jnp.where(matches, gates[:, :, None], jnp.float32(0.0)), axis=1)
    present = jnp.any(matches, axis=1)
    capacity = HOTCAP * (TOKENS // TOK_DEV)
    grad_tokens = jnp.zeros((TOKENS, D), jnp.float32)
    gate_parts = []
    up_parts = []
    down_parts = []
    for expert in range(FLIGHT):
        index_list = jnp.nonzero(present[:, expert], size=capacity, fill_value=0)[0].astype(jnp.int32)
        live_count = jnp.sum(present[:, expert].astype(jnp.int32))
        valid_rows = jnp.arange(capacity, dtype=jnp.int32) < live_count
        row_gate = jnp.where(valid_rows, expert_gate[index_list, expert], jnp.float32(0.0))
        in_tokens = tokens[index_list]
        in_scaled = (row_gate[:, None] * grad_out[index_list].astype(jnp.float32)).astype(jnp.bfloat16)
        gate_rows = gate_weight[expert * FF:(expert + 1) * FF]
        up_rows = up_weight[expert * FF:(expert + 1) * FF]
        down_rows = down_weight[expert * FF:(expert + 1) * FF]
        pre_gate = jnp.dot(in_tokens, gate_rows.T, preferred_element_type=jnp.float32)
        pre_up = jnp.dot(in_tokens, up_rows.T, preferred_element_type=jnp.float32)
        sigmoid_gate = jax.nn.sigmoid(pre_gate)
        swish_gate = pre_gate * sigmoid_gate
        activated = (swish_gate * pre_up).astype(jnp.bfloat16)
        grad_act = jnp.dot(in_scaled, down_rows.T, preferred_element_type=jnp.float32)
        grad_pre_gate = (grad_act * pre_up * sigmoid_gate * (1.0 + pre_gate * (1.0 - sigmoid_gate))).astype(jnp.bfloat16)
        grad_pre_up = (grad_act * swish_gate).astype(jnp.bfloat16)
        gate_parts.append(jnp.dot(grad_pre_gate.T, in_tokens, preferred_element_type=jnp.float32))
        up_parts.append(jnp.dot(grad_pre_up.T, in_tokens, preferred_element_type=jnp.float32))
        down_parts.append(jnp.dot(activated.T, in_scaled, preferred_element_type=jnp.float32))
        total_rows = jnp.zeros((capacity, D), jnp.float32)
        for block_index in range(SPLIT):
            columns = slice(block_index * HD, (block_index + 1) * HD)
            partial_block = jnp.dot(grad_pre_gate[:, columns], gate_rows[columns], preferred_element_type=jnp.float32)
            partial_block = partial_block + jnp.dot(grad_pre_up[:, columns], up_rows[columns], preferred_element_type=jnp.float32)
            rounded = lax.optimization_barrier(partial_block.astype(jnp.bfloat16))
            total_rows = total_rows + rounded.astype(jnp.float32)
        grad_tokens = grad_tokens.at[index_list].add(total_rows)
    grad_gate = jnp.concatenate(gate_parts, axis=0).astype(jnp.bfloat16)
    grad_up = jnp.concatenate(up_parts, axis=0).astype(jnp.bfloat16)
    grad_down = jnp.concatenate(down_parts, axis=0).astype(jnp.bfloat16)
    return (grad_tokens.astype(jnp.bfloat16), grad_gate, grad_up, grad_down)
```

```python
import jax
import jax.numpy as jnp
from jax import lax
from jax.experimental import pallas as pl
from jax.experimental.pallas import tpu as pltpu
from jax.sharding import PartitionSpec as P

FLIGHT = 8
HOTCAP = 8
F32 = jnp.float32
BF16 = jnp.bfloat16
MIB = 1 << 20


def expert_pass(in_tokens, in_scaled, gate_rows, up_rows, down_rows):
    pre_gate = jnp.einsum("nd,hd->nh", in_tokens, gate_rows, preferred_element_type=jnp.float32)
    pre_up = jnp.einsum("nd,hd->nh", in_tokens, up_rows, preferred_element_type=jnp.float32)
    sigmoid_gate = jax.nn.sigmoid(pre_gate)
    swish_gate = pre_gate * sigmoid_gate
    activated = (swish_gate * pre_up).astype(jnp.bfloat16)
    grad_act = jnp.einsum("nd,hd->nh", in_scaled, down_rows, preferred_element_type=jnp.float32)
    grad_pre_gate = (
        grad_act * pre_up * sigmoid_gate * (1.0 + pre_gate * (1.0 - sigmoid_gate))
    ).astype(jnp.bfloat16)
    grad_pre_up = (grad_act * swish_gate).astype(jnp.bfloat16)
    gate_term = jnp.einsum(
        "nh,nd->hd", grad_pre_gate, in_tokens, preferred_element_type=jnp.float32
    )
    up_term = jnp.einsum("nh,nd->hd", grad_pre_up, in_tokens, preferred_element_type=jnp.float32)
    down_term = jnp.einsum("nh,nd->hd", activated, in_scaled, preferred_element_type=jnp.float32)
    partials = jnp.dot(grad_pre_gate, gate_rows, preferred_element_type=jnp.float32)
    partials = (
        partials + jnp.dot(grad_pre_up, up_rows, preferred_element_type=jnp.float32)
    ).astype(jnp.bfloat16)
    return (partials, (gate_term, up_term, down_term))


def per_device_general(
    tokens, grad_out, routing, gates, modality, hot_experts, gate_weight, up_weight, down_weight
):
    tok_count, model_width = tokens.shape
    top_count = routing.shape[1]
    hot_count = hot_experts.shape[0]
    devices = lax.axis_size("expert")
    split_count = devices // FLIGHT
    position = lax.broadcasted_iota(jnp.int32, (tok_count, top_count), 1)
    pinned_slot = position - (top_count - hot_count)
    pick_table = pinned_slot[:, :, None] == jnp.arange(hot_count, dtype=jnp.int32)[None, None, :]
    hot_pick = jnp.sum(jnp.where(pick_table, hot_experts[None, None, :], 0), axis=2)
    pinned = (modality[:, None] == 1) & (pinned_slot >= 0)
    chosen = jnp.where(pinned, hot_pick, routing)
    matches = chosen[:, :, None] == jnp.arange(FLIGHT, dtype=jnp.int32)[None, None, :]
    expert_gate = jnp.sum(jnp.where(matches, gates[:, :, None], 0.0), axis=1)
    present = jnp.any(matches, axis=1)
    placed = jnp.cumsum(present.astype(jnp.int32), axis=0) - 1
    slot_ids = jnp.arange(HOTCAP, dtype=jnp.int32)
    chooser = (placed.T[:, None, :] == slot_ids[None, :, None]) & present.T[:, None, :]
    picker = chooser.astype(jnp.bfloat16)
    picked = jnp.einsum("scr,rd->scd", picker, tokens, preferred_element_type=jnp.float32).astype(
        jnp.bfloat16
    )
    picked_grad = jnp.einsum("scr,rd->scd", picker, grad_out, preferred_element_type=jnp.float32)
    slot_gate = jnp.sum(jnp.where(chooser, expert_gate.T[:, None, :], 0.0), axis=2)
    scaled = (picked_grad * slot_gate[:, :, None]).astype(jnp.bfloat16)
    send_shape = (devices, HOTCAP, model_width)

    def replicate_rows(block_data):
        widened = jnp.broadcast_to(block_data[:, None], (FLIGHT, split_count, HOTCAP, model_width))
        return widened.reshape(send_shape)

    got_tokens, got_scaled = (
        lax.all_to_all(replicate_rows(picked), "expert", split_axis=0, concat_axis=0, tiled=True),
        lax.all_to_all(replicate_rows(scaled), "expert", split_axis=0, concat_axis=0, tiled=True),
    )
    partials, grad_terms = expert_pass(
        got_tokens.reshape(-1, model_width),
        got_scaled.reshape(-1, model_width),
        gate_weight,
        up_weight,
        down_weight,
    )
    returned = lax.all_to_all(
        partials.reshape(send_shape), "expert", split_axis=0, concat_axis=0, tiled=True
    )
    returned = returned.reshape(FLIGHT, split_count, HOTCAP, model_width)
    grad_tokens = jnp.einsum(
        "fcr,fpcd->rd", chooser.astype(jnp.bfloat16), returned, preferred_element_type=jnp.float32
    )
    summed = tuple(
        lax.psum_scatter(term, "dp", scatter_dimension=0, tiled=True) for term in grad_terms
    )
    return (grad_tokens.astype(jnp.bfloat16),) + tuple(term.astype(jnp.bfloat16) for term in summed)


def pick_rows(where, hot_experts, tokens, grad_out, routing, gates, modality):
    tok_count, width = tokens.shape
    top_count = routing.shape[1]
    hot_count = hot_experts.shape[0]
    slots = FLIGHT * HOTCAP
    steps = 2

    def kernel(where_ref, hot_ref, tok_ref, gout_ref, route_ref, gate_ref, mod_ref, *rest):
        msgs = rest[:FLIGHT]
        choose_ref, slot_gate_ref = rest[FLIGHT:]

        @pl.when(pl.program_id(0) == 0)
        def _():
            position = lax.broadcasted_iota(jnp.int32, (top_count, tok_count), 0)
            hot_pick = jnp.zeros((top_count, tok_count), jnp.int32)
            for j in range(hot_count):
                hot_pick = jnp.where(
                    position == top_count - hot_count + j, hot_ref[j], hot_pick
                )
            pinned = (mod_ref[...] == 1) & (position >= top_count - hot_count)
            chosen = jnp.where(pinned, hot_pick, route_ref[...])
            expert = lax.broadcasted_iota(jnp.int32, (FLIGHT, top_count, tok_count), 0)
            expert = expert ^ where_ref[0]
            matches = chosen[None] == expert
            expert_gate = jnp.sum(jnp.where(matches, gate_ref[...][None], 0.0), axis=1)
            present = jnp.sum(jnp.where(matches, 1.0, 0.0), axis=1)
            before = lax.broadcasted_iota(jnp.int32, (tok_count, tok_count), 0)
            after = lax.broadcasted_iota(jnp.int32, (tok_count, tok_count), 1)
            upto = jnp.where(before <= after, 1.0, 0.0).astype(BF16)
            placed = jnp.dot(present.astype(BF16), upto, preferred_element_type=F32)
            slot = lax.broadcasted_iota(jnp.int32, (FLIGHT, HOTCAP, tok_count), 1) + 1
            slot_hit = placed[:, None, :].astype(jnp.int32) == slot
            chooser = slot_hit & (present[:, None, :] > 0.0)
            picker = jnp.where(chooser, 1.0, 0.0).reshape(slots, tok_count)
            choose_ref[...] = picker.astype(BF16)
            picked_gate = jnp.where(chooser, expert_gate[:, None, :], 0.0)
            slot_gate_ref[...] = jnp.sum(
                picked_gate.reshape(slots, tok_count), axis=1, keepdims=True
            )

        picker = choose_ref[...]
        picked = jnp.dot(picker, tok_ref[...], preferred_element_type=F32)
        scaled = jnp.dot(picker, gout_ref[...], preferred_element_type=F32) * slot_gate_ref[...]
        for s in range(FLIGHT):
            rows = slice(s * HOTCAP, (s + 1) * HOTCAP)
            msgs[s][0] = picked[rows].astype(BF16)
            msgs[s][1] = scaled[rows].astype(BF16)

    block = width // steps
    whole = lambda i, *_: (0, 0)
    column = lambda i, *_: (0, i)
    out = pl.pallas_call(
        kernel,
        out_shape=[jax.ShapeDtypeStruct((2, HOTCAP, width), BF16)] * FLIGHT
        + [jax.ShapeDtypeStruct((slots, tok_count), BF16)],
        grid_spec=pltpu.PrefetchScalarGridSpec(
            num_scalar_prefetch=2,
            grid=(steps,),
            in_specs=[
                pl.BlockSpec((tok_count, block), column),
                pl.BlockSpec((tok_count, block), column),
                pl.BlockSpec((top_count, tok_count), whole),
                pl.BlockSpec((top_count, tok_count), whole),
                pl.BlockSpec((1, tok_count), whole),
            ],
            out_specs=[pl.BlockSpec((2, HOTCAP, block), lambda i, *_: (0, 0, i))] * FLIGHT
            + [pl.BlockSpec((slots, tok_count), whole)],
            scratch_shapes=[pltpu.VMEM((slots, 1), F32)],
        ),
        cost_estimate=pl.CostEstimate(
            flops=4 * slots * tok_count * width,
            bytes_accessed=4 * (slots + tok_count) * width,
            transcendentals=0,
        ),
        name="pick_rows",
    )(where, hot_experts, tokens, grad_out, routing.T, gates.T, modality[None, :])
    return out[:FLIGHT], out[FLIGHT]


def activation_grads(where, own, other, gate_weight, up_weight, down_weight):
    _, rows, width = own.shape
    half = gate_weight.shape[0] // 2
    tile = min(256, half)
    steps = half // tile
    nt = (((1,), (1,)), ((), ()))

    def kernel(where_ref, own_ref, other_ref, g_ref, u_ref, w_ref, *rest):
        dh_ref, du_ref, act_ref, mine_ref, theirs_ref, tok, scl, acc = rest
        step = pl.program_id(0)

        @pl.when(step == 0)
        def _():
            tok[:rows] = own_ref[0]
            tok[rows:] = other_ref[0]
            scl[:rows] = own_ref[1]
            scl[rows:] = other_ref[1]

        h = lax.dot_general(tok[...], g_ref[...], nt, preferred_element_type=F32)
        u = lax.dot_general(tok[...], u_ref[...], nt, preferred_element_type=F32)
        da = lax.dot_general(scl[...], w_ref[...], nt, preferred_element_type=F32)
        sig = jax.nn.sigmoid(h)
        swish = h * sig
        act_ref[...] = (swish * u).astype(BF16)
        dh = (da * u * sig * (1.0 + h * (1.0 - sig))).astype(BF16)
        du = (da * swish).astype(BF16)
        dh_ref[...] = dh
        du_ref[...] = du
        part = jnp.dot(dh, g_ref[...], preferred_element_type=F32)
        part += jnp.dot(du, u_ref[...], preferred_element_type=F32)

        @pl.when(step == 0)
        def _():
            acc[...] = part

        @pl.when(step > 0)
        def _():
            acc[...] += part

        @pl.when(step == steps - 1)
        def _():
            mine_ref[...] = acc[:rows]
            theirs_ref[...] = acc[rows:].astype(BF16)

    fixed3 = lambda i, w: (0, 0, 0)
    fixed2 = lambda i, w: (0, 0)
    weight = pl.BlockSpec((tile, width), lambda i, w: (w[1] * steps + i, 0))
    hidden = pl.BlockSpec((2 * rows, tile), lambda i, w: (0, i))
    return pl.pallas_call(
        kernel,
        out_shape=[jax.ShapeDtypeStruct((2 * rows, half), BF16)] * 3
        + [
            jax.ShapeDtypeStruct((rows, width), F32),
            jax.ShapeDtypeStruct((rows, width), BF16),
        ],
        grid_spec=pltpu.PrefetchScalarGridSpec(
            num_scalar_prefetch=1,
            grid=(steps,),
            in_specs=[
                pl.BlockSpec((2, rows, width), fixed3),
                pl.BlockSpec((2, rows, width), fixed3),
                weight,
                weight,
                weight,
            ],
            out_specs=[
                hidden,
                hidden,
                hidden,
                pl.BlockSpec((rows, width), fixed2),
                pl.BlockSpec((rows, width), fixed2),
            ],
            scratch_shapes=[
                pltpu.VMEM((2 * rows, width), BF16),
                pltpu.VMEM((2 * rows, width), BF16),
                pltpu.VMEM((2 * rows, width), F32),
            ],
        ),
        compiler_params=pltpu.CompilerParams(vmem_limit_bytes=48 * MIB),
        cost_estimate=pl.CostEstimate(
            flops=20 * rows * half * width,
            bytes_accessed=6 * half * width,
            transcendentals=2 * rows * half,
        ),
        name="activation_grads",
    )(where, own, other, gate_weight, up_weight, down_weight)


def weight_grads(own, other, dh, du, act):
    _, rows, width = own.shape
    half = dh.shape[1]
    tile = min(256, half)
    steps = half // tile
    tn = (((0,), (0,)), ((), ()))

    def kernel(own_ref, other_ref, dh_ref, du_ref, act_ref, gg_ref, gu_ref, gd_ref, tok, scl):
        @pl.when(pl.program_id(0) == 0)
        def _():
            tok[:rows] = own_ref[0]
            tok[rows:] = other_ref[0]
            scl[:rows] = own_ref[1]
            scl[rows:] = other_ref[1]

        for left, right, out in (
            (dh_ref, tok, gg_ref),
            (du_ref, tok, gu_ref),
            (act_ref, scl, gd_ref),
        ):
            out[...] = lax.dot_general(
                left[...], right[...], tn, preferred_element_type=F32
            ).astype(BF16)

    fixed3 = lambda i: (0, 0, 0)
    hidden = pl.BlockSpec((2 * rows, tile), lambda i: (0, i))
    out_block = pl.BlockSpec((tile, width), lambda i: (i, 0))
    return pl.pallas_call(
        kernel,
        out_shape=[jax.ShapeDtypeStruct((half, width), BF16)] * 3,
        grid=(steps,),
        in_specs=[
            pl.BlockSpec((2, rows, width), fixed3),
            pl.BlockSpec((2, rows, width), fixed3),
            hidden,
            hidden,
            hidden,
        ],
        out_specs=[out_block] * 3,
        scratch_shapes=[
            pltpu.VMEM((2 * rows, width), BF16),
            pltpu.VMEM((2 * rows, width), BF16),
        ],
        compiler_params=pltpu.CompilerParams(vmem_limit_bytes=48 * MIB),
        cost_estimate=pl.CostEstimate(
            flops=12 * rows * half * width,
            bytes_accessed=6 * half * width,
            transcendentals=0,
        ),
        name="weight_grads",
    )(own, other, dh, du, act)


def per_device(
    tokens, grad_out, routing, gates, modality, hot_experts, gate_weight, up_weight, down_weight
):
    where = jnp.stack([lax.axis_index("expert"), lax.axis_index("dp")]).astype(jnp.int32)
    swap = [(0, 1), (1, 0)]

    def hop(block, s):
        if s == 0:
            return block
        return lax.ppermute(block, "expert", [(i, i ^ s) for i in range(FLIGHT)])

    msgs, picker = pick_rows(where, hot_experts, tokens, grad_out, routing, gates, modality)
    got = [None] * FLIGHT
    for s in reversed(range(FLIGHT)):
        got[s] = hop(msgs[s], s)
    own = jnp.concatenate(got, axis=1)
    other = lax.ppermute(own, "dp", swap)
    dh, du, act, mine, theirs = activation_grads(
        where, own, other, gate_weight, up_weight, down_weight
    )
    pieces = (mine + lax.ppermute(theirs, "dp", swap).astype(F32)).astype(BF16)
    back = [None] * FLIGHT
    for s in reversed(range(FLIGHT)):
        back[s] = hop(pieces[s * HOTCAP : (s + 1) * HOTCAP], s)
    grad_gate, grad_up, grad_down = weight_grads(own, other, dh, du, act)
    grad_tokens = lax.dot_general(
        picker,
        jnp.concatenate(back, axis=0),
        (((0,), (0,)), ((), ())),
        preferred_element_type=F32,
    ).astype(BF16)
    return grad_tokens, grad_gate, grad_up, grad_down


def solution(mesh):
    sizes = dict(mesh.shape)
    token_spec = P(("groups", "expert", "dp"), None)
    in_specs = (
        token_spec,
        token_spec,
        token_spec,
        token_spec,
        P(("groups", "expert", "dp")),
        P("groups"),
        P("expert", None),
        P("expert", None),
        P("expert", None),
    )
    paired = sizes["expert"] == FLIGHT and sizes["dp"] == 2
    return jax.shard_map(
        per_device if paired else per_device_general,
        mesh=mesh,
        in_specs=in_specs,
        out_specs=(token_spec,) * 4,
        check_vma=False,
    )
```

```python
import jax
import jax.numpy as jnp
from jax import lax
from jax.experimental import pallas as pl
from jax.experimental.pallas import tpu as pltpu
from jax.sharding import PartitionSpec as P

FLIGHT = 8
HOTCAP = 8
F32 = jnp.float32
BF16 = jnp.bfloat16
MIB = 1 << 20


def expert_pass(in_tokens, in_scaled, gate_rows, up_rows, down_rows):
    pre_gate = jnp.einsum("nd,hd->nh", in_tokens, gate_rows, preferred_element_type=jnp.float32)
    pre_up = jnp.einsum("nd,hd->nh", in_tokens, up_rows, preferred_element_type=jnp.float32)
    sigmoid_gate = jax.nn.sigmoid(pre_gate)
    swish_gate = pre_gate * sigmoid_gate
    activated = (swish_gate * pre_up).astype(jnp.bfloat16)
    grad_act = jnp.einsum("nd,hd->nh", in_scaled, down_rows, preferred_element_type=jnp.float32)
    grad_pre_gate = (
        grad_act * pre_up * sigmoid_gate * (1.0 + pre_gate * (1.0 - sigmoid_gate))
    ).astype(jnp.bfloat16)
    grad_pre_up = (grad_act * swish_gate).astype(jnp.bfloat16)
    gate_term = jnp.einsum(
        "nh,nd->hd", grad_pre_gate, in_tokens, preferred_element_type=jnp.float32
    )
    up_term = jnp.einsum("nh,nd->hd", grad_pre_up, in_tokens, preferred_element_type=jnp.float32)
    down_term = jnp.einsum("nh,nd->hd", activated, in_scaled, preferred_element_type=jnp.float32)
    partials = jnp.dot(grad_pre_gate, gate_rows, preferred_element_type=jnp.float32)
    partials = (
        partials + jnp.dot(grad_pre_up, up_rows, preferred_element_type=jnp.float32)
    ).astype(jnp.bfloat16)
    return (partials, (gate_term, up_term, down_term))


def per_device_general(
    tokens, grad_out, routing, gates, modality, hot_experts, gate_weight, up_weight, down_weight
):
    tok_count, model_width = tokens.shape
    top_count = routing.shape[1]
    hot_count = hot_experts.shape[0]
    devices = lax.axis_size("expert")
    split_count = devices // FLIGHT
    position = lax.broadcasted_iota(jnp.int32, (tok_count, top_count), 1)
    pinned_slot = position - (top_count - hot_count)
    pick_table = pinned_slot[:, :, None] == jnp.arange(hot_count, dtype=jnp.int32)[None, None, :]
    hot_pick = jnp.sum(jnp.where(pick_table, hot_experts[None, None, :], 0), axis=2)
    pinned = (modality[:, None] == 1) & (pinned_slot >= 0)
    chosen = jnp.where(pinned, hot_pick, routing)
    matches = chosen[:, :, None] == jnp.arange(FLIGHT, dtype=jnp.int32)[None, None, :]
    expert_gate = jnp.sum(jnp.where(matches, gates[:, :, None], 0.0), axis=1)
    present = jnp.any(matches, axis=1)
    placed = jnp.cumsum(present.astype(jnp.int32), axis=0) - 1
    slot_ids = jnp.arange(HOTCAP, dtype=jnp.int32)
    chooser = (placed.T[:, None, :] == slot_ids[None, :, None]) & present.T[:, None, :]
    picker = chooser.astype(jnp.bfloat16)
    picked = jnp.einsum("scr,rd->scd", picker, tokens, preferred_element_type=jnp.float32).astype(
        jnp.bfloat16
    )
    picked_grad = jnp.einsum("scr,rd->scd", picker, grad_out, preferred_element_type=jnp.float32)
    slot_gate = jnp.sum(jnp.where(chooser, expert_gate.T[:, None, :], 0.0), axis=2)
    scaled = (picked_grad * slot_gate[:, :, None]).astype(jnp.bfloat16)
    send_shape = (devices, HOTCAP, model_width)

    def replicate_rows(block_data):
        widened = jnp.broadcast_to(block_data[:, None], (FLIGHT, split_count, HOTCAP, model_width))
        return widened.reshape(send_shape)

    got_tokens, got_scaled = (
        lax.all_to_all(replicate_rows(picked), "expert", split_axis=0, concat_axis=0, tiled=True),
        lax.all_to_all(replicate_rows(scaled), "expert", split_axis=0, concat_axis=0, tiled=True),
    )
    partials, grad_terms = expert_pass(
        got_tokens.reshape(-1, model_width),
        got_scaled.reshape(-1, model_width),
        gate_weight,
        up_weight,
        down_weight,
    )
    returned = lax.all_to_all(
        partials.reshape(send_shape), "expert", split_axis=0, concat_axis=0, tiled=True
    )
    returned = returned.reshape(FLIGHT, split_count, HOTCAP, model_width)
    grad_tokens = jnp.einsum(
        "fcr,fpcd->rd", chooser.astype(jnp.bfloat16), returned, preferred_element_type=jnp.float32
    )
    summed = tuple(
        lax.psum_scatter(term, "dp", scatter_dimension=0, tiled=True) for term in grad_terms
    )
    return (grad_tokens.astype(jnp.bfloat16),) + tuple(term.astype(jnp.bfloat16) for term in summed)


HOPS = (7, 4, 2, 1)


def pick_tokens(where, hot_experts, tokens, routing, gates, modality):
    tok_count, width = tokens.shape
    top_count = routing.shape[1]
    hot_count = hot_experts.shape[0]
    slots = FLIGHT * HOTCAP
    hops = len(HOPS)

    def kernel(where_ref, hot_ref, tok_ref, route_ref, gate_ref, mod_ref, *outs):
        keeps = outs[:hops]
        give_ref, choose_ref, slot_gate_ref = outs[hops:]
        position = lax.broadcasted_iota(jnp.int32, (top_count, tok_count), 0)
        hot_pick = jnp.zeros((top_count, tok_count), jnp.int32)
        for j in range(hot_count):
            hot_pick = jnp.where(position == top_count - hot_count + j, hot_ref[j], hot_pick)
        pinned = (mod_ref[...] == 1) & (position >= top_count - hot_count)
        chosen = jnp.where(pinned, hot_pick, route_ref[...])
        index = lax.broadcasted_iota(jnp.int32, (FLIGHT, top_count, tok_count), 0)
        hop = jnp.zeros_like(index)
        for k, value in enumerate(HOPS):
            hop = jnp.where(index % hops == k, value, hop)
        expert = hop ^ (index // hops) ^ where_ref[0] ^ where_ref[1]
        matches = chosen[None] == expert
        expert_gate = jnp.sum(jnp.where(matches, gate_ref[...][None], 0.0), axis=1)
        present = jnp.sum(jnp.where(matches, 1.0, 0.0), axis=1)
        before = lax.broadcasted_iota(jnp.int32, (tok_count, tok_count), 0)
        after = lax.broadcasted_iota(jnp.int32, (tok_count, tok_count), 1)
        upto = jnp.where(before <= after, 1.0, 0.0).astype(BF16)
        placed = jnp.dot(present.astype(BF16), upto, preferred_element_type=F32)
        slot = lax.broadcasted_iota(jnp.int32, (FLIGHT, HOTCAP, tok_count), 1) + 1
        slot_hit = placed[:, None, :].astype(jnp.int32) == slot
        chooser = slot_hit & (present[:, None, :] > 0.0)
        picker = jnp.where(chooser, 1.0, 0.0).reshape(slots, tok_count).astype(BF16)
        choose_ref[...] = picker
        picked_gate = jnp.where(chooser, expert_gate[:, None, :], 0.0)
        slot_gate_ref[...] = jnp.sum(picked_gate.reshape(slots, tok_count), axis=1, keepdims=True)
        picked = jnp.dot(picker, tok_ref[...], preferred_element_type=F32)
        for k in range(hops):
            keeps[k][...] = picked[k * HOTCAP : (k + 1) * HOTCAP].astype(BF16)
        give_ref[...] = picked[hops * HOTCAP :].astype(BF16)

    smem = pl.BlockSpec(memory_space=pltpu.SMEM)
    vmem = pl.BlockSpec(memory_space=pltpu.VMEM)
    out = pl.pallas_call(
        kernel,
        out_shape=[jax.ShapeDtypeStruct((HOTCAP, width), BF16)] * hops
        + [
            jax.ShapeDtypeStruct((hops * HOTCAP, width), BF16),
            jax.ShapeDtypeStruct((slots, tok_count), BF16),
            jax.ShapeDtypeStruct((slots, 1), F32),
        ],
        in_specs=[smem, smem, vmem, vmem, vmem, vmem],
        out_specs=[vmem] * (hops + 3),
        cost_estimate=pl.CostEstimate(
            flops=2 * slots * tok_count * width,
            bytes_accessed=2 * (slots + tok_count) * width,
            transcendentals=0,
        ),
        name="pick_tokens",
    )(where, hot_experts, tokens, routing.T, gates.T, modality[None, :])
    return out[:hops], out[hops], out[hops + 1], out[hops + 2]


def pick_scaled(grad_out, picker, slot_gate):
    tok_count, width = grad_out.shape
    slots = picker.shape[0]
    hops = len(HOPS)

    def kernel(gout_ref, choose_ref, slot_gate_ref, *outs):
        scaled = jnp.dot(choose_ref[...], gout_ref[...], preferred_element_type=F32)
        scaled = scaled * slot_gate_ref[...]
        for k in range(hops):
            outs[k][...] = scaled[k * HOTCAP : (k + 1) * HOTCAP].astype(BF16)
        outs[hops][...] = scaled[hops * HOTCAP :].astype(BF16)

    vmem = pl.BlockSpec(memory_space=pltpu.VMEM)
    out = pl.pallas_call(
        kernel,
        out_shape=[jax.ShapeDtypeStruct((HOTCAP, width), BF16)] * hops
        + [jax.ShapeDtypeStruct((hops * HOTCAP, width), BF16)],
        in_specs=[vmem] * 3,
        out_specs=[vmem] * (hops + 1),
        cost_estimate=pl.CostEstimate(
            flops=2 * slots * tok_count * width,
            bytes_accessed=2 * (slots + tok_count) * width,
            transcendentals=0,
        ),
        name="pick_scaled",
    )(grad_out, picker, slot_gate)
    return out[:hops], out[hops]


NT = (((1,), (1,)), ((), ()))
TN = (((0,), (0,)), ((), ()))


def pre_activations(where, own, other, gate_weight, up_weight):
    rows, width = own.shape
    half = gate_weight.shape[0] // 2
    tile = min(256, half)
    steps = half // tile

    def kernel(where_ref, own_ref, other_ref, g_ref, u_ref, h_ref, u_out_ref, tok):
        @pl.when(pl.program_id(0) == 0)
        def _():
            tok[:rows] = own_ref[...]
            tok[rows:] = other_ref[...]

        h_ref[...] = lax.dot_general(g_ref[...], tok[...], NT, preferred_element_type=F32)
        u_out_ref[...] = lax.dot_general(u_ref[...], tok[...], NT, preferred_element_type=F32)

    fixed = lambda i, w: (0, 0)
    weight = pl.BlockSpec((tile, width), lambda i, w: (w[1] * steps + i, 0))
    hidden = pl.BlockSpec((tile, 2 * rows), lambda i, w: (i, 0))
    return pl.pallas_call(
        kernel,
        out_shape=[jax.ShapeDtypeStruct((half, 2 * rows), F32)] * 2,
        grid_spec=pltpu.PrefetchScalarGridSpec(
            num_scalar_prefetch=1,
            grid=(steps,),
            in_specs=[pl.BlockSpec((rows, width), fixed)] * 2 + [weight] * 2,
            out_specs=[hidden] * 2,
            scratch_shapes=[pltpu.VMEM((2 * rows, width), BF16)],
        ),
        compiler_params=pltpu.CompilerParams(vmem_limit_bytes=50 * MIB),
        cost_estimate=pl.CostEstimate(
            flops=8 * rows * half * width,
            bytes_accessed=4 * half * width,
            transcendentals=0,
        ),
        name="pre_activations",
    )(where, own, other, gate_weight, up_weight)


def activation_grads(where, own, other, h, u, gate_weight, up_weight, down_weight):
    rows, width = own.shape
    half = gate_weight.shape[0] // 2
    tile = min(256, half)
    steps = half // tile

    def kernel(where_ref, own_ref, other_ref, h_in, u_in, g_ref, u_ref, w_ref, *rest):
        dh_ref, du_ref, act_ref, mine_ref, theirs_ref, scl, acc = rest
        step = pl.program_id(0)

        @pl.when(step == 0)
        def _():
            scl[:rows] = own_ref[...]
            scl[rows:] = other_ref[...]

        da = lax.dot_general(w_ref[...], scl[...], NT, preferred_element_type=F32)
        pre, up = h_in[...], u_in[...]
        sig = jax.nn.sigmoid(pre)
        swish = pre * sig
        act_ref[...] = (swish * up).astype(BF16)
        dh = (da * up * sig * (1.0 + pre * (1.0 - sig))).astype(BF16)
        du = (da * swish).astype(BF16)
        dh_ref[...] = dh
        du_ref[...] = du
        part = lax.dot_general(dh, g_ref[...], TN, preferred_element_type=F32)
        part += lax.dot_general(du, u_ref[...], TN, preferred_element_type=F32)

        @pl.when(step == 0)
        def _():
            acc[...] = part

        @pl.when(step > 0)
        def _():
            acc[...] += part

        @pl.when(step == steps - 1)
        def _():
            mine_ref[...] = acc[:rows]
            theirs_ref[...] = acc[rows:].astype(BF16)

    fixed = lambda i, w: (0, 0)
    weight = pl.BlockSpec((tile, width), lambda i, w: (w[1] * steps + i, 0))
    hidden = pl.BlockSpec((tile, 2 * rows), lambda i, w: (i, 0))
    full = pl.BlockSpec((rows, width), fixed)
    return pl.pallas_call(
        kernel,
        out_shape=[jax.ShapeDtypeStruct((half, 2 * rows), BF16)] * 3
        + [
            jax.ShapeDtypeStruct((rows, width), F32),
            jax.ShapeDtypeStruct((rows, width), BF16),
        ],
        grid_spec=pltpu.PrefetchScalarGridSpec(
            num_scalar_prefetch=1,
            grid=(steps,),
            in_specs=[full, full, hidden, hidden, weight, weight, weight],
            out_specs=[hidden, hidden, hidden, full, full],
            scratch_shapes=[
                pltpu.VMEM((2 * rows, width), BF16),
                pltpu.VMEM((2 * rows, width), F32),
            ],
        ),
        compiler_params=pltpu.CompilerParams(vmem_limit_bytes=50 * MIB),
        cost_estimate=pl.CostEstimate(
            flops=12 * rows * half * width,
            bytes_accessed=6 * half * width,
            transcendentals=2 * rows * half,
        ),
        name="activation_grads",
    )(where, own, other, h, u, gate_weight, up_weight, down_weight)


def weight_grads(own_tok, other_tok, own_scl, other_scl, dh, du, act):
    rows, width = own_tok.shape
    half = dh.shape[0]
    tile = min(256, half)
    steps = half // tile

    def kernel(own_t, other_t, own_s, other_s, dh_ref, du_ref, act_ref, *rest):
        gg_ref, gu_ref, gd_ref, tok, scl = rest

        @pl.when(pl.program_id(0) == 0)
        def _():
            tok[:rows] = own_t[...]
            tok[rows:] = other_t[...]
            scl[:rows] = own_s[...]
            scl[rows:] = other_s[...]

        for left, right, out in (
            (dh_ref, tok, gg_ref),
            (du_ref, tok, gu_ref),
            (act_ref, scl, gd_ref),
        ):
            out[...] = jnp.dot(left[...], right[...], preferred_element_type=F32).astype(BF16)

    full = pl.BlockSpec((rows, width), lambda i: (0, 0))
    hidden = pl.BlockSpec((tile, 2 * rows), lambda i: (i, 0))
    return pl.pallas_call(
        kernel,
        out_shape=[jax.ShapeDtypeStruct((half, width), BF16)] * 3,
        grid=(steps,),
        in_specs=[full] * 4 + [hidden] * 3,
        out_specs=[pl.BlockSpec((tile, width), lambda i: (i, 0))] * 3,
        scratch_shapes=[pltpu.VMEM((2 * rows, width), BF16)] * 2,
        compiler_params=pltpu.CompilerParams(vmem_limit_bytes=50 * MIB),
        cost_estimate=pl.CostEstimate(
            flops=12 * rows * half * width,
            bytes_accessed=6 * half * width,
            transcendentals=0,
        ),
        name="weight_grads",
    )(own_tok, other_tok, own_scl, other_scl, dh, du, act)


def per_device(
    tokens, grad_out, routing, gates, modality, hot_experts, gate_weight, up_weight, down_weight
):
    where = jnp.stack([lax.axis_index("expert"), lax.axis_index("dp")]).astype(jnp.int32)
    hops = len(HOPS)

    def swap(block):
        return lax.ppermute(block, "dp", [(0, 1), (1, 0)])

    def travel(block, hop):
        moves = [
            (2 * i + c, 2 * (i ^ hop ^ c) + c) for i in range(FLIGHT) for c in range(2)
        ]
        return lax.ppermute(block, ("expert", "dp"), moves)

    def dispatch(keeps, give):
        taken = swap(give)
        got = []
        for k, hop in enumerate(HOPS):
            theirs = taken[k * HOTCAP : (k + 1) * HOTCAP]
            got.append(travel(jnp.concatenate([keeps[k], theirs], axis=0), hop))
        return got

    tok_keeps, tok_give, picker, slot_gate = pick_tokens(
        where, hot_experts, tokens, routing, gates, modality
    )
    scl_keeps, scl_give = pick_scaled(grad_out, picker, slot_gate)
    own_tok = jnp.concatenate(dispatch(tok_keeps, tok_give), axis=0)
    got_scl = dispatch(scl_keeps, scl_give)
    other_tok = swap(own_tok)
    h, u = pre_activations(where, own_tok, other_tok, gate_weight, up_weight)
    got_scl, h, u = lax.optimization_barrier((got_scl, h, u))
    own_scl = jnp.concatenate(got_scl, axis=0)
    other_scl = swap(own_scl)
    dh, du, act, mine, theirs = activation_grads(
        where, own_scl, other_scl, h, u, gate_weight, up_weight, down_weight
    )
    pieces = (mine + swap(theirs).astype(F32)).astype(BF16)
    back = []
    for k, hop in enumerate(HOPS):
        back.append(travel(pieces[2 * k * HOTCAP : 2 * (k + 1) * HOTCAP], hop))
    grad_gate, grad_up, grad_down = weight_grads(
        own_tok, other_tok, own_scl, other_scl, dh, du, act
    )
    back, grad_gate, grad_up, grad_down = lax.optimization_barrier(
        (back, grad_gate, grad_up, grad_down)
    )
    kept = jnp.concatenate([block[:HOTCAP] for block in back], axis=0)
    given = swap(jnp.concatenate([block[HOTCAP:] for block in back], axis=0))
    grad_tokens = lax.dot_general(
        picker, jnp.concatenate([kept, given], axis=0), TN, preferred_element_type=F32
    ).astype(BF16)
    return grad_tokens, grad_gate, grad_up, grad_down


def solution(mesh):
    sizes = dict(mesh.shape)
    token_spec = P(("groups", "expert", "dp"), None)
    in_specs = (
        token_spec,
        token_spec,
        token_spec,
        token_spec,
        P(("groups", "expert", "dp")),
        P("groups"),
        P("expert", None),
        P("expert", None),
        P("expert", None),
    )
    paired = sizes["expert"] == FLIGHT and sizes["dp"] == 2
    return jax.shard_map(
        per_device if paired else per_device_general,
        mesh=mesh,
        in_specs=in_specs,
        out_specs=(token_spec,) * 4,
        check_vma=False,
    )
```

```python
import jax
import jax.numpy as jnp
from jax import lax
from jax.experimental import pallas as pl
from jax.experimental.pallas import tpu as pltpu
from jax.sharding import PartitionSpec as P

FLIGHT = 8
HOTCAP = 8
F32 = jnp.float32
BF16 = jnp.bfloat16
MIB = 1 << 20


def expert_pass(in_tokens, in_scaled, gate_rows, up_rows, down_rows):
    pre_gate = jnp.einsum("nd,hd->nh", in_tokens, gate_rows, preferred_element_type=jnp.float32)
    pre_up = jnp.einsum("nd,hd->nh", in_tokens, up_rows, preferred_element_type=jnp.float32)
    sigmoid_gate = jax.nn.sigmoid(pre_gate)
    swish_gate = pre_gate * sigmoid_gate
    activated = (swish_gate * pre_up).astype(jnp.bfloat16)
    grad_act = jnp.einsum("nd,hd->nh", in_scaled, down_rows, preferred_element_type=jnp.float32)
    grad_pre_gate = (
        grad_act * pre_up * sigmoid_gate * (1.0 + pre_gate * (1.0 - sigmoid_gate))
    ).astype(jnp.bfloat16)
    grad_pre_up = (grad_act * swish_gate).astype(jnp.bfloat16)
    gate_term = jnp.einsum(
        "nh,nd->hd", grad_pre_gate, in_tokens, preferred_element_type=jnp.float32
    )
    up_term = jnp.einsum("nh,nd->hd", grad_pre_up, in_tokens, preferred_element_type=jnp.float32)
    down_term = jnp.einsum("nh,nd->hd", activated, in_scaled, preferred_element_type=jnp.float32)
    partials = jnp.dot(grad_pre_gate, gate_rows, preferred_element_type=jnp.float32)
    partials = (
        partials + jnp.dot(grad_pre_up, up_rows, preferred_element_type=jnp.float32)
    ).astype(jnp.bfloat16)
    return (partials, (gate_term, up_term, down_term))


def per_device_general(
    tokens, grad_out, routing, gates, modality, hot_experts, gate_weight, up_weight, down_weight
):
    tok_count, model_width = tokens.shape
    top_count = routing.shape[1]
    hot_count = hot_experts.shape[0]
    devices = lax.axis_size("expert")
    split_count = devices // FLIGHT
    position = lax.broadcasted_iota(jnp.int32, (tok_count, top_count), 1)
    pinned_slot = position - (top_count - hot_count)
    pick_table = pinned_slot[:, :, None] == jnp.arange(hot_count, dtype=jnp.int32)[None, None, :]
    hot_pick = jnp.sum(jnp.where(pick_table, hot_experts[None, None, :], 0), axis=2)
    pinned = (modality[:, None] == 1) & (pinned_slot >= 0)
    chosen = jnp.where(pinned, hot_pick, routing)
    matches = chosen[:, :, None] == jnp.arange(FLIGHT, dtype=jnp.int32)[None, None, :]
    expert_gate = jnp.sum(jnp.where(matches, gates[:, :, None], 0.0), axis=1)
    present = jnp.any(matches, axis=1)
    placed = jnp.cumsum(present.astype(jnp.int32), axis=0) - 1
    slot_ids = jnp.arange(HOTCAP, dtype=jnp.int32)
    chooser = (placed.T[:, None, :] == slot_ids[None, :, None]) & present.T[:, None, :]
    picker = chooser.astype(jnp.bfloat16)
    picked = jnp.einsum("scr,rd->scd", picker, tokens, preferred_element_type=jnp.float32).astype(
        jnp.bfloat16
    )
    picked_grad = jnp.einsum("scr,rd->scd", picker, grad_out, preferred_element_type=jnp.float32)
    slot_gate = jnp.sum(jnp.where(chooser, expert_gate.T[:, None, :], 0.0), axis=2)
    scaled = (picked_grad * slot_gate[:, :, None]).astype(jnp.bfloat16)
    send_shape = (devices, HOTCAP, model_width)

    def replicate_rows(block_data):
        widened = jnp.broadcast_to(block_data[:, None], (FLIGHT, split_count, HOTCAP, model_width))
        return widened.reshape(send_shape)

    got_tokens, got_scaled = (
        lax.all_to_all(replicate_rows(picked), "expert", split_axis=0, concat_axis=0, tiled=True),
        lax.all_to_all(replicate_rows(scaled), "expert", split_axis=0, concat_axis=0, tiled=True),
    )
    partials, grad_terms = expert_pass(
        got_tokens.reshape(-1, model_width),
        got_scaled.reshape(-1, model_width),
        gate_weight,
        up_weight,
        down_weight,
    )
    returned = lax.all_to_all(
        partials.reshape(send_shape), "expert", split_axis=0, concat_axis=0, tiled=True
    )
    returned = returned.reshape(FLIGHT, split_count, HOTCAP, model_width)
    grad_tokens = jnp.einsum(
        "fcr,fpcd->rd", chooser.astype(jnp.bfloat16), returned, preferred_element_type=jnp.float32
    )
    summed = tuple(
        lax.psum_scatter(term, "dp", scatter_dimension=0, tiled=True) for term in grad_terms
    )
    return (grad_tokens.astype(jnp.bfloat16),) + tuple(term.astype(jnp.bfloat16) for term in summed)


HOPS = (7, 4, 2, 1)
FAR = 2
CARRIED = len(HOPS) * HOTCAP
NT = (((1,), (1,)), ((), ()))
SMEM = pl.BlockSpec(memory_space=pltpu.SMEM)
VMEM = pl.BlockSpec(memory_space=pltpu.VMEM)
HBM = pl.BlockSpec(memory_space=pltpu.HBM)


def route(hot_experts, routing, gates, modality, tokens, grad_out):
    tok_count, top_count = routing.shape
    hot_count = hot_experts.shape[0]
    slots = FLIGHT * HOTCAP
    hops = len(HOPS)

    def kernel(hot_ref, route_ref, gate_ref, mod_ref, tok_in, gout_in, *rest):
        choose_ref, keep_ref, give_ref, tok_ref, gout_ref, sem = rest
        loads = (
            pltpu.make_async_copy(tok_in, tok_ref, sem.at[0]),
            pltpu.make_async_copy(gout_in, gout_ref, sem.at[1]),
        )
        for load in loads:
            load.start()
        position = lax.broadcasted_iota(jnp.int32, (top_count, tok_count), 0)
        hot_pick = jnp.zeros((top_count, tok_count), jnp.int32)
        for j in range(hot_count):
            hot_pick = jnp.where(position == top_count - hot_count + j, hot_ref[j], hot_pick)
        pinned = (mod_ref[...] == 1) & (position >= top_count - hot_count)
        chosen = jnp.where(pinned, hot_pick, route_ref[...])
        index = lax.broadcasted_iota(jnp.int32, (FLIGHT, top_count, tok_count), 0)
        hop = jnp.zeros_like(index)
        for k, value in enumerate(HOPS):
            hop = jnp.where(index % hops == k, value, hop)
        expert = hop ^ (index // hops) ^ lax.axis_index("expert") ^ lax.axis_index("dp")
        matches = chosen[None] == expert
        expert_gate = jnp.sum(jnp.where(matches, gate_ref[...][None], 0.0), axis=1)
        present = jnp.sum(jnp.where(matches, 1.0, 0.0), axis=1)
        before = lax.broadcasted_iota(jnp.int32, (tok_count, tok_count), 0)
        after = lax.broadcasted_iota(jnp.int32, (tok_count, tok_count), 1)
        upto = jnp.where(before <= after, 1.0, 0.0).astype(BF16)
        placed = jnp.dot(present.astype(BF16), upto, preferred_element_type=F32)
        slot = lax.broadcasted_iota(jnp.int32, (FLIGHT, HOTCAP, tok_count), 1) + 1
        slot_hit = placed[:, None, :].astype(jnp.int32) == slot
        chooser = slot_hit & (present[:, None, :] > 0.0)
        picker = jnp.where(chooser, 1.0, 0.0).reshape(slots, tok_count)
        gated = jnp.where(chooser, expert_gate[:, None, :], 0.0).reshape(slots, tok_count)
        choose_ref[...] = picker.astype(BF16)
        keep_ref[...] = gated[:CARRIED]
        give_ref[...] = gated[CARRIED:]
        for load in loads:
            load.wait()

    return pl.pallas_call(
        kernel,
        out_shape=[
            pltpu.VMEM((slots, tok_count), BF16),
            pltpu.VMEM((CARRIED, tok_count), F32),
            pltpu.VMEM((slots - CARRIED, tok_count), F32),
            pltpu.VMEM(tokens.shape, BF16),
            pltpu.VMEM(grad_out.shape, BF16),
        ],
        in_specs=[SMEM, VMEM, VMEM, VMEM, HBM, HBM],
        out_specs=[VMEM] * 5,
        scratch_shapes=[pltpu.SemaphoreType.DMA((2,))],
        name="route",
    )(
        hot_experts,
        routing.T,
        gates.T,
        modality[None, :],
        pltpu.with_memory_space_constraint(tokens, pltpu.HBM),
        pltpu.with_memory_space_constraint(grad_out, pltpu.HBM),
    )


def pick(slots, tokens, grads, parts, work, name):
    tok_count, width = tokens[0].shape
    sources = [rows for rows in (tokens, grads) if rows is not None]

    def kernel(*refs):
        outs = refs[2 + 2 * len(sources) :]
        for core in range(2):
            gated = refs[core][...]
            picker = jnp.where(gated != 0.0, 1.0, 0.0).astype(BF16)
            first = min(k for k, _ in parts) * HOTCAP
            picker = picker[first:]
            gate = jnp.sum(gated[first:], axis=1, keepdims=True)
            rows = [
                jnp.dot(picker, refs[2 + 2 * n + core][...], preferred_element_type=F32)
                for n in range(len(sources))
            ]
            if grads is not None:
                rows[1] = rows[1] * gate
            for (k, carried), out in zip(parts, outs):
                slot = slice(k * HOTCAP - first, (k + 1) * HOTCAP - first)
                for place, n in enumerate(carried):
                    start = (2 * place + core) * HOTCAP
                    out[start : start + HOTCAP] = rows[n][slot].astype(BF16)

    return pl.pallas_call(
        kernel,
        out_shape=[
            pltpu.VMEM((2 * HOTCAP * len(carried), width), BF16) for _, carried in parts
        ],
        in_specs=[VMEM] * (2 + 2 * len(sources)),
        out_specs=[VMEM] * len(parts),
        compiler_params=pltpu.CompilerParams(vmem_limit_bytes=16 * MIB),
        cost_estimate=pl.CostEstimate(
            flops=4 * work * CARRIED * tok_count * width,
            bytes_accessed=4 * work * (CARRIED + tok_count) * width,
            transcendentals=0,
        ),
        name=name,
    )(*slots, *(block for pair in sources for block in pair))


def pre_activations(own, other, gate_weight, up_weight, down_weight):
    rows, width = own.shape
    half = gate_weight.shape[0] // 2
    tile = min(256, half)
    steps = half // tile

    def kernel(own_ref, other_ref, g_in, u_in, w_in, h_ref, up_ref, g_ref, u_ref, w_ref, *rest):
        columns, sem = rest
        first = pl.multiple_of(lax.axis_index("dp") * half, half)
        order = [(lane, i) for i in range(steps) for lane in (0, 1)]
        order += [(2, i) for i in range(steps)]

        def load(lane, i):
            source, target = ((g_in, g_ref), (u_in, u_ref), (w_in, w_ref))[lane]
            return pltpu.make_async_copy(
                source.at[pl.ds(first + i * tile, tile)],
                target.at[pl.ds(i * tile, tile)],
                sem.at[lane, i],
            )

        depth = 3
        for lane, i in order[:depth]:
            load(lane, i).start()
        columns[:, :rows] = own_ref[...].T
        columns[:, rows:] = other_ref[...].T
        for n, (lane, i) in enumerate(order):
            load(lane, i).wait()
            if n + depth < len(order):
                load(*order[n + depth]).start()
            if lane < 2:
                part = slice(i * tile, (i + 1) * tile)
                weight, out = ((g_ref, h_ref), (u_ref, up_ref))[lane]
                out[part] = jnp.dot(weight[part], columns[...], preferred_element_type=F32)

    return pl.pallas_call(
        kernel,
        out_shape=[pltpu.VMEM((half, 2 * rows), F32)] * 2
        + [pltpu.VMEM((half, width), BF16)] * 3,
        in_specs=[VMEM, VMEM, HBM, HBM, HBM],
        out_specs=[VMEM] * 5,
        scratch_shapes=[
            pltpu.VMEM((width, 2 * rows), BF16),
            pltpu.SemaphoreType.DMA((3, steps)),
        ],
        compiler_params=pltpu.CompilerParams(vmem_limit_bytes=12 * MIB),
        cost_estimate=pl.CostEstimate(flops=1000, bytes_accessed=1000, transcendentals=0),
        name="pre_activations",
    )(
        own,
        other,
        *(
            pltpu.with_memory_space_constraint(weight, pltpu.HBM)
            for weight in (gate_weight, up_weight, down_weight)
        ),
    )


def activation_grads(own, other, h, u, gate_half, up_half, down_half):
    rows, width = own.shape
    half = h.shape[0]
    tile = min(256, half)
    chunk = 512 if width % 512 == 0 else width

    def kernel(own_ref, other_ref, h_ref, up_ref, g_ref, u_ref, w_ref, *rest):
        dh_ref, du_ref, act_ref, mine_ref, theirs_ref, scl, dh_rows, du_rows = rest
        scl[:rows] = own_ref[...]
        scl[rows:] = other_ref[...]
        for i in range(half // tile):
            part = slice(i * tile, (i + 1) * tile)
            da = lax.dot_general(w_ref[part], scl[...], NT, preferred_element_type=F32)
            pre, up = h_ref[part], up_ref[part]
            sig = jax.nn.sigmoid(pre)
            swish = pre * sig
            act_ref[part] = (swish * up).astype(BF16)
            dh = (da * up * sig * (1.0 + pre * (1.0 - sig))).astype(BF16)
            du = (da * swish).astype(BF16)
            dh_ref[part] = dh
            du_ref[part] = du
            dh_rows[:, part] = dh.T
            du_rows[:, part] = du.T
        for c in range(0, width, chunk):
            cols = slice(c, c + chunk)
            piece = jnp.dot(dh_rows[...], g_ref[:, cols], preferred_element_type=F32)
            piece += jnp.dot(du_rows[...], u_ref[:, cols], preferred_element_type=F32)
            mine_ref[:, cols] = piece[:rows]
            theirs_ref[:, cols] = piece[rows:].astype(BF16)

    return pl.pallas_call(
        kernel,
        out_shape=[pltpu.VMEM((half, 2 * rows), BF16)] * 3
        + [pltpu.VMEM((rows, width), F32), pltpu.VMEM((rows, width), BF16)],
        in_specs=[VMEM] * 7,
        out_specs=[VMEM] * 5,
        scratch_shapes=[
            pltpu.VMEM((2 * rows, width), BF16),
            pltpu.VMEM((2 * rows, half), BF16),
            pltpu.VMEM((2 * rows, half), BF16),
        ],
        compiler_params=pltpu.CompilerParams(vmem_limit_bytes=12 * MIB),
        cost_estimate=pl.CostEstimate(
            flops=12 * rows * half * width,
            bytes_accessed=6 * half * width,
            transcendentals=2 * rows * half,
        ),
        name="activation_grads",
    )(own, other, h, u, gate_half, up_half, down_half)


def weight_grads(own, other, lefts, name):
    rows, width = own.shape
    half = lefts[0].shape[0]
    tile = min(256, half)
    count = len(lefts)

    def kernel(own_ref, other_ref, *rest):
        sides, outs, both = rest[:count], rest[count : 2 * count], rest[2 * count]

        @pl.when(pl.program_id(0) == 0)
        def _():
            both[:rows] = own_ref[...]
            both[rows:] = other_ref[...]

        for left, out in zip(sides, outs):
            out[...] = jnp.dot(left[...], both[...], preferred_element_type=F32).astype(BF16)

    full = pl.BlockSpec((rows, width), lambda i: (0, 0))
    hidden = pl.BlockSpec((tile, 2 * rows), lambda i: (i, 0))
    return pl.pallas_call(
        kernel,
        out_shape=[jax.ShapeDtypeStruct((half, width), BF16)] * count,
        grid=(half // tile,),
        in_specs=[full] * 2 + [hidden] * count,
        out_specs=[pl.BlockSpec((tile, width), lambda i: (i, 0))] * count,
        scratch_shapes=[pltpu.VMEM((2 * rows, width), BF16)],
        compiler_params=pltpu.CompilerParams(vmem_limit_bytes=24 * MIB),
        cost_estimate=pl.CostEstimate(
            flops=4 * count * rows * half * width,
            bytes_accessed=2 * count * half * width,
            transcendentals=0,
        ),
        name=name,
    )(own, other, *lefts)


def per_device(
    tokens, grad_out, routing, gates, modality, hot_experts, gate_weight, up_weight, down_weight
):
    def swap(block):
        return lax.ppermute(block, "dp", [(0, 1), (1, 0)])

    def travel(block, hop):
        moves = [
            (2 * i + c, 2 * (i ^ hop ^ c) + c) for i in range(FLIGHT) for c in range(2)
        ]
        return lax.ppermute(block, ("expert", "dp"), moves)

    picker, keep, give, my_tokens, my_grads = route(
        hot_experts, routing, gates, modality, tokens, grad_out
    )
    slots = (keep, swap(give))
    tok_rows = (my_tokens, swap(tokens))
    grad_rows = (my_grads, swap(grad_out))
    hops = range(len(HOPS))
    tok_msgs = pick(slots, tok_rows, None, [(k, (0,)) for k in hops[:FAR]], 1, "pick_far")
    rest = [(k, (1,)) for k in hops[:FAR]] + [(k, (0, 1)) for k in hops[FAR:]]
    rest_msgs = pick(slots, tok_rows, grad_rows, rest, 2, "pick_rest")
    scl_msgs, near_msgs = rest_msgs[:FAR], rest_msgs[FAR:]
    got_tok = [travel(m, hop) for m, hop in zip(tok_msgs, HOPS)]
    got_near = [travel(m, hop) for m, hop in zip(near_msgs, HOPS[FAR:])]
    got_scl = [travel(m, hop) for m, hop in zip(scl_msgs, HOPS)]
    half = 2 * HOTCAP
    own_tok = jnp.concatenate(got_tok + [block[:half] for block in got_near], axis=0)
    other_tok = swap(own_tok)
    pre = pre_activations(own_tok, other_tok, gate_weight, up_weight, down_weight)
    got_scl, pre = lax.optimization_barrier((got_scl, pre))
    own_scl = jnp.concatenate(got_scl + [block[half:] for block in got_near], axis=0)
    other_scl = swap(own_scl)
    dh, du, act, mine, theirs = activation_grads(own_scl, other_scl, *pre)
    (grad_down,) = weight_grads(own_scl, other_scl, [act], "down_grad")
    added, grad_down = lax.optimization_barrier((swap(theirs), grad_down))
    pieces = (mine + added.astype(F32)).astype(BF16)
    back = [
        travel(pieces[2 * k * HOTCAP : 2 * (k + 1) * HOTCAP], hop) for k, hop in enumerate(HOPS)
    ]
    grad_gate, grad_up = weight_grads(own_tok, other_tok, [dh, du], "gate_up_grads")
    back, grad_gate, grad_up = lax.optimization_barrier((back, grad_gate, grad_up))
    kept = jnp.concatenate([block[:HOTCAP] for block in back], axis=0)
    given = swap(jnp.concatenate([block[HOTCAP:] for block in back], axis=0))
    grad_tokens = lax.dot_general(
        picker,
        jnp.concatenate([kept, given], axis=0),
        (((0,), (0,)), ((), ())),
        preferred_element_type=F32,
    ).astype(BF16)
    return grad_tokens, grad_gate, grad_up, grad_down


def solution(mesh):
    sizes = dict(mesh.shape)
    token_spec = P(("groups", "expert", "dp"), None)
    in_specs = (
        token_spec,
        token_spec,
        token_spec,
        token_spec,
        P(("groups", "expert", "dp")),
        P("groups"),
        P("expert", None),
        P("expert", None),
        P("expert", None),
    )
    paired = sizes["expert"] == FLIGHT and sizes["dp"] == 2
    return jax.shard_map(
        per_device if paired else per_device_general,
        mesh=mesh,
        in_specs=in_specs,
        out_specs=(token_spec,) * 4,
        check_vma=False,
    )
```

```python
import jax
import jax.numpy as jnp
from jax import lax
from jax.experimental import pallas as pl
from jax.experimental.pallas import tpu as pltpu
from jax.sharding import PartitionSpec as P

FLIGHT = 8
HOTCAP = 8
F32 = jnp.float32
BF16 = jnp.bfloat16
MIB = 1 << 20


def expert_pass(in_tokens, in_scaled, gate_rows, up_rows, down_rows):
    pre_gate = jnp.einsum("nd,hd->nh", in_tokens, gate_rows, preferred_element_type=jnp.float32)
    pre_up = jnp.einsum("nd,hd->nh", in_tokens, up_rows, preferred_element_type=jnp.float32)
    sigmoid_gate = jax.nn.sigmoid(pre_gate)
    swish_gate = pre_gate * sigmoid_gate
    activated = (swish_gate * pre_up).astype(jnp.bfloat16)
    grad_act = jnp.einsum("nd,hd->nh", in_scaled, down_rows, preferred_element_type=jnp.float32)
    grad_pre_gate = (
        grad_act * pre_up * sigmoid_gate * (1.0 + pre_gate * (1.0 - sigmoid_gate))
    ).astype(jnp.bfloat16)
    grad_pre_up = (grad_act * swish_gate).astype(jnp.bfloat16)
    gate_term = jnp.einsum(
        "nh,nd->hd", grad_pre_gate, in_tokens, preferred_element_type=jnp.float32
    )
    up_term = jnp.einsum("nh,nd->hd", grad_pre_up, in_tokens, preferred_element_type=jnp.float32)
    down_term = jnp.einsum("nh,nd->hd", activated, in_scaled, preferred_element_type=jnp.float32)
    partials = jnp.dot(grad_pre_gate, gate_rows, preferred_element_type=jnp.float32)
    partials = (
        partials + jnp.dot(grad_pre_up, up_rows, preferred_element_type=jnp.float32)
    ).astype(jnp.bfloat16)
    return (partials, (gate_term, up_term, down_term))


def per_device_general(
    tokens, grad_out, routing, gates, modality, hot_experts, gate_weight, up_weight, down_weight
):
    tok_count, model_width = tokens.shape
    top_count = routing.shape[1]
    hot_count = hot_experts.shape[0]
    devices = lax.axis_size("expert")
    split_count = devices // FLIGHT
    position = lax.broadcasted_iota(jnp.int32, (tok_count, top_count), 1)
    pinned_slot = position - (top_count - hot_count)
    pick_table = pinned_slot[:, :, None] == jnp.arange(hot_count, dtype=jnp.int32)[None, None, :]
    hot_pick = jnp.sum(jnp.where(pick_table, hot_experts[None, None, :], 0), axis=2)
    pinned = (modality[:, None] == 1) & (pinned_slot >= 0)
    chosen = jnp.where(pinned, hot_pick, routing)
    matches = chosen[:, :, None] == jnp.arange(FLIGHT, dtype=jnp.int32)[None, None, :]
    expert_gate = jnp.sum(jnp.where(matches, gates[:, :, None], 0.0), axis=1)
    present = jnp.any(matches, axis=1)
    placed = jnp.cumsum(present.astype(jnp.int32), axis=0) - 1
    slot_ids = jnp.arange(HOTCAP, dtype=jnp.int32)
    chooser = (placed.T[:, None, :] == slot_ids[None, :, None]) & present.T[:, None, :]
    picker = chooser.astype(jnp.bfloat16)
    picked = jnp.einsum("scr,rd->scd", picker, tokens, preferred_element_type=jnp.float32).astype(
        jnp.bfloat16
    )
    picked_grad = jnp.einsum("scr,rd->scd", picker, grad_out, preferred_element_type=jnp.float32)
    slot_gate = jnp.sum(jnp.where(chooser, expert_gate.T[:, None, :], 0.0), axis=2)
    scaled = (picked_grad * slot_gate[:, :, None]).astype(jnp.bfloat16)
    send_shape = (devices, HOTCAP, model_width)

    def replicate_rows(block_data):
        widened = jnp.broadcast_to(block_data[:, None], (FLIGHT, split_count, HOTCAP, model_width))
        return widened.reshape(send_shape)

    got_tokens, got_scaled = (
        lax.all_to_all(replicate_rows(picked), "expert", split_axis=0, concat_axis=0, tiled=True),
        lax.all_to_all(replicate_rows(scaled), "expert", split_axis=0, concat_axis=0, tiled=True),
    )
    partials, grad_terms = expert_pass(
        got_tokens.reshape(-1, model_width),
        got_scaled.reshape(-1, model_width),
        gate_weight,
        up_weight,
        down_weight,
    )
    returned = lax.all_to_all(
        partials.reshape(send_shape), "expert", split_axis=0, concat_axis=0, tiled=True
    )
    returned = returned.reshape(FLIGHT, split_count, HOTCAP, model_width)
    grad_tokens = jnp.einsum(
        "fcr,fpcd->rd", chooser.astype(jnp.bfloat16), returned, preferred_element_type=jnp.float32
    )
    summed = tuple(
        lax.psum_scatter(term, "dp", scatter_dimension=0, tiled=True) for term in grad_terms
    )
    return (grad_tokens.astype(jnp.bfloat16),) + tuple(term.astype(jnp.bfloat16) for term in summed)


HOPS = (7, 4, 2, 1)
CARRIED = len(HOPS) * HOTCAP
NT = (((1,), (1,)), ((), ()))
SMEM = pl.BlockSpec(memory_space=pltpu.SMEM)
VMEM = pl.BlockSpec(memory_space=pltpu.VMEM)
HBM = pl.BlockSpec(memory_space=pltpu.HBM)


def route(hot_experts, routing, gates, modality, tokens, grad_out):
    tok_count, top_count = routing.shape
    hot_count = hot_experts.shape[0]
    slots = FLIGHT * HOTCAP
    hops = len(HOPS)

    def kernel(hot_ref, route_ref, gate_ref, mod_ref, tok_in, gout_in, *rest):
        choose_ref, keep_ref, give_ref, tok_ref, gout_ref, sem = rest
        loads = (
            pltpu.make_async_copy(tok_in, tok_ref, sem.at[0]),
            pltpu.make_async_copy(gout_in, gout_ref, sem.at[1]),
        )
        for load in loads:
            load.start()
        position = lax.broadcasted_iota(jnp.int32, (top_count, tok_count), 0)
        hot_pick = jnp.zeros((top_count, tok_count), jnp.int32)
        for j in range(hot_count):
            hot_pick = jnp.where(position == top_count - hot_count + j, hot_ref[j], hot_pick)
        pinned = (mod_ref[...] == 1) & (position >= top_count - hot_count)
        chosen = jnp.where(pinned, hot_pick, route_ref[...])
        index = lax.broadcasted_iota(jnp.int32, (FLIGHT, top_count, tok_count), 0)
        hop = jnp.zeros_like(index)
        for k, value in enumerate(HOPS):
            hop = jnp.where(index % hops == k, value, hop)
        expert = hop ^ (index // hops) ^ lax.axis_index("expert") ^ lax.axis_index("dp")
        matches = chosen[None] == expert
        expert_gate = jnp.sum(jnp.where(matches, gate_ref[...][None], 0.0), axis=1)
        present = jnp.sum(jnp.where(matches, 1.0, 0.0), axis=1)
        before = lax.broadcasted_iota(jnp.int32, (tok_count, tok_count), 0)
        after = lax.broadcasted_iota(jnp.int32, (tok_count, tok_count), 1)
        upto = jnp.where(before <= after, 1.0, 0.0).astype(BF16)
        placed = jnp.dot(present.astype(BF16), upto, preferred_element_type=F32)
        slot = lax.broadcasted_iota(jnp.int32, (FLIGHT, HOTCAP, tok_count), 1) + 1
        slot_hit = placed[:, None, :].astype(jnp.int32) == slot
        chooser = slot_hit & (present[:, None, :] > 0.0)
        picker = jnp.where(chooser, 1.0, 0.0).reshape(slots, tok_count)
        gated = jnp.where(chooser, expert_gate[:, None, :], 0.0).reshape(slots, tok_count)
        choose_ref[...] = picker.astype(BF16)
        keep_ref[...] = gated[:CARRIED]
        give_ref[...] = gated[CARRIED:]
        for load in loads:
            load.wait()

    return pl.pallas_call(
        kernel,
        out_shape=[
            pltpu.VMEM((slots, tok_count), BF16),
            pltpu.VMEM((CARRIED, tok_count), F32),
            pltpu.VMEM((slots - CARRIED, tok_count), F32),
            pltpu.VMEM(tokens.shape, BF16),
            pltpu.VMEM(grad_out.shape, BF16),
        ],
        in_specs=[SMEM, VMEM, VMEM, VMEM, HBM, HBM],
        out_specs=[VMEM] * 5,
        scratch_shapes=[pltpu.SemaphoreType.DMA((2,))],
        name="route",
    )(
        hot_experts,
        routing.T,
        gates.T,
        modality[None, :],
        pltpu.with_memory_space_constraint(tokens, pltpu.HBM),
        pltpu.with_memory_space_constraint(grad_out, pltpu.HBM),
    )


def pick(mine, theirs, my_tokens, their_tokens, my_grads, their_grads):
    tok_count, width = my_tokens.shape

    def kernel(mine_ref, theirs_ref, my_tok, their_tok, my_grad, their_grad, *outs):
        for core, slot_ref, tok_ref, grad_ref in (
            (0, mine_ref, my_tok, my_grad),
            (1, theirs_ref, their_tok, their_grad),
        ):
            gated = slot_ref[...]
            picker = jnp.where(gated != 0.0, 1.0, 0.0).astype(BF16)
            rows = jnp.dot(picker, tok_ref[...], preferred_element_type=F32)
            scaled = jnp.dot(picker, grad_ref[...], preferred_element_type=F32)
            scaled = scaled * jnp.sum(gated, axis=1, keepdims=True)
            for k, out in enumerate(outs):
                slot = slice(k * HOTCAP, (k + 1) * HOTCAP)
                out[core * HOTCAP : (core + 1) * HOTCAP] = rows[slot].astype(BF16)
                out[(core + 2) * HOTCAP : (core + 3) * HOTCAP] = scaled[slot].astype(BF16)

    return pl.pallas_call(
        kernel,
        out_shape=[pltpu.VMEM((4 * HOTCAP, width), BF16)] * len(HOPS),
        in_specs=[VMEM] * 6,
        out_specs=[VMEM] * len(HOPS),
        compiler_params=pltpu.CompilerParams(vmem_limit_bytes=16 * MIB),
        cost_estimate=pl.CostEstimate(
            flops=8 * CARRIED * tok_count * width,
            bytes_accessed=8 * (CARRIED + tok_count) * width,
            transcendentals=0,
        ),
        name="pick",
    )(mine, theirs, my_tokens, their_tokens, my_grads, their_grads)


def load_weights(*weights):
    half = weights[0].shape[0] // 2
    width = weights[0].shape[1]
    count = len(weights)

    def kernel(*refs):
        first = pl.multiple_of(lax.axis_index("dp") * half, half)
        loads = [
            pltpu.make_async_copy(
                refs[i].at[pl.ds(first, half)], refs[count + i], refs[2 * count].at[i]
            )
            for i in range(count)
        ]
        for load in loads:
            load.start()
        for load in loads:
            load.wait()

    return pl.pallas_call(
        kernel,
        out_shape=[pltpu.VMEM((half, width), BF16)] * count,
        in_specs=[HBM] * count,
        out_specs=[VMEM] * count,
        scratch_shapes=[pltpu.SemaphoreType.DMA((count,))],
        compiler_params=pltpu.CompilerParams(vmem_limit_bytes=2 * MIB),
        cost_estimate=pl.CostEstimate(
            flops=0, bytes_accessed=4 * count * half * width, transcendentals=0
        ),
        name="load_weights",
    )(*(pltpu.with_memory_space_constraint(weight, pltpu.HBM) for weight in weights))


def activation_grads(blocks, gate_half, up_half, down_half):
    width = blocks[0].shape[1]
    rows = 2 * HOTCAP * len(HOPS)
    half = gate_half.shape[0]
    tile = min(256, half)
    chunk = 512 if width % 512 == 0 else width

    def kernel(*refs):
        ins, refs = refs[: len(blocks)], refs[len(blocks) :]
        g_ref, u_ref, w_ref, tok_ref, scl_ref, dh_ref, du_ref, act_ref = refs[:8]
        mine_ref, theirs_ref, tok_cols, scl_cols, dh_rows, du_rows = refs[8:]
        message = 2 * HOTCAP
        place = 0
        for block in ins:
            for start in range(0, block.shape[0], 2 * message):
                tok_ref[place : place + message] = block[start : start + message]
                scl_ref[place : place + message] = block[start + message : start + 2 * message]
                place += message
        tok_cols[...] = tok_ref[...].T
        scl_cols[...] = scl_ref[...].T
        for i in range(half // tile):
            part = slice(i * tile, (i + 1) * tile)
            pre = jnp.dot(g_ref[part], tok_cols[...], preferred_element_type=F32)
            up = jnp.dot(u_ref[part], tok_cols[...], preferred_element_type=F32)
            da = jnp.dot(w_ref[part], scl_cols[...], preferred_element_type=F32)
            sig = jax.nn.sigmoid(pre)
            swish = pre * sig
            act_ref[part] = (swish * up).astype(BF16)
            dh = (da * up * sig * (1.0 + pre * (1.0 - sig))).astype(BF16)
            du = (da * swish).astype(BF16)
            dh_ref[part] = dh
            du_ref[part] = du
            dh_rows[:, part] = dh.T
            du_rows[:, part] = du.T
        for c in range(0, width, chunk):
            cols = slice(c, c + chunk)
            piece = jnp.dot(dh_rows[...], g_ref[:, cols], preferred_element_type=F32)
            piece += jnp.dot(du_rows[...], u_ref[:, cols], preferred_element_type=F32)
            mine_ref[:, cols] = piece[:rows]
            theirs_ref[:, cols] = piece[rows:].astype(BF16)

    return pl.pallas_call(
        kernel,
        out_shape=[pltpu.VMEM((2 * rows, width), BF16)] * 2
        + [pltpu.VMEM((half, 2 * rows), BF16)] * 3
        + [pltpu.VMEM((rows, width), F32), pltpu.VMEM((rows, width), BF16)],
        in_specs=[VMEM] * (len(blocks) + 3),
        out_specs=[VMEM] * 7,
        scratch_shapes=[
            pltpu.VMEM((width, 2 * rows), BF16),
            pltpu.VMEM((width, 2 * rows), BF16),
            pltpu.VMEM((2 * rows, half), BF16),
            pltpu.VMEM((2 * rows, half), BF16),
        ],
        compiler_params=pltpu.CompilerParams(vmem_limit_bytes=12 * MIB),
        cost_estimate=pl.CostEstimate(
            flops=20 * rows * half * width,
            bytes_accessed=6 * half * width,
            transcendentals=2 * rows * half,
        ),
        name="activation_grads",
    )(*blocks, gate_half, up_half, down_half)


def weight_grad(rows, left, name):
    count, width = rows.shape
    half = left.shape[0]
    chunk = 512 if width % 512 == 0 else width

    def kernel(rows_ref, left_ref, out_ref):
        for c in range(0, width, chunk):
            cols = slice(c, c + chunk)
            out_ref[:, cols] = jnp.dot(
                left_ref[...], rows_ref[:, cols], preferred_element_type=F32
            ).astype(BF16)

    return pl.pallas_call(
        kernel,
        out_shape=pltpu.VMEM((half, width), BF16),
        in_specs=[VMEM, VMEM],
        out_specs=VMEM,
        compiler_params=pltpu.CompilerParams(vmem_limit_bytes=8 * MIB),
        cost_estimate=pl.CostEstimate(
            flops=2 * count * half * width, bytes_accessed=2 * half * width, transcendentals=0
        ),
        name=name,
    )(rows, left)


def gate_up_grads(rows, gate_left, up_left, down):
    count, width = rows.shape
    half = gate_left.shape[0]
    chunk = 512 if width % 512 == 0 else width

    def kernel(rows_ref, gate_ref, up_ref, down_ref, gate_out, down_out, up_out, held, sem):
        copies = [pltpu.make_async_copy(down_ref, down_out, sem.at[0])]
        copies[0].start()
        for n, c in enumerate(range(0, width, chunk)):
            cols = slice(c, c + chunk)
            held[:, cols] = jnp.dot(
                gate_ref[...], rows_ref[:, cols], preferred_element_type=F32
            ).astype(BF16)
            copies.append(
                pltpu.make_async_copy(held.at[:, cols], gate_out.at[:, cols], sem.at[1 + n])
            )
            copies[-1].start()
        for c in range(0, width, chunk):
            cols = slice(c, c + chunk)
            up_out[:, cols] = jnp.dot(
                up_ref[...], rows_ref[:, cols], preferred_element_type=F32
            ).astype(BF16)
        for copy in copies:
            copy.wait()

    full = jax.ShapeDtypeStruct((half, width), BF16)
    return pl.pallas_call(
        kernel,
        out_shape=[full, full, pltpu.VMEM((half, width), BF16)],
        in_specs=[VMEM] * 4,
        out_specs=[HBM, HBM, VMEM],
        scratch_shapes=[
            pltpu.VMEM((half, width), BF16),
            pltpu.SemaphoreType.DMA((1 + width // chunk,)),
        ],
        compiler_params=pltpu.CompilerParams(vmem_limit_bytes=12 * MIB),
        cost_estimate=pl.CostEstimate(
            flops=4 * count * half * width, bytes_accessed=4 * half * width, transcendentals=0
        ),
        name="gate_up_grads",
    )(rows, gate_left, up_left, down)


def write_first(block):
    rows = block.shape[0] // 2

    def kernel(block_ref, out, sem):
        copy = pltpu.make_async_copy(block_ref.at[pl.ds(0, rows)], out.at[pl.ds(0, rows)], sem)
        copy.start()
        copy.wait()

    return pl.pallas_call(
        kernel,
        out_shape=jax.ShapeDtypeStruct(block.shape, block.dtype),
        in_specs=[VMEM],
        out_specs=HBM,
        scratch_shapes=[pltpu.SemaphoreType.DMA],
        compiler_params=pltpu.CompilerParams(vmem_limit_bytes=2 * MIB),
        cost_estimate=pl.CostEstimate(
            flops=0, bytes_accessed=2 * block.size, transcendentals=0
        ),
        name="write_first",
    )(block)


def combine(picker, returned, block, written):
    slots, tok_count = picker.shape
    width = returned.shape[1]
    rows = block.shape[0] // 2
    chunk = 512 if width % 512 == 0 else width

    def kernel(pick_ref, back_ref, block_ref, _, sum_out, block_out, held, sem):
        rest = pl.ds(rows, rows)
        copies = [pltpu.make_async_copy(block_ref.at[rest], block_out.at[rest], sem.at[0])]
        copies[0].start()
        chooser = pick_ref[...].T
        for n, c in enumerate(range(0, width, chunk)):
            cols = slice(c, c + chunk)
            held[:, cols] = jnp.dot(
                chooser, back_ref[:, cols], preferred_element_type=F32
            ).astype(BF16)
            copies.append(
                pltpu.make_async_copy(held.at[:, cols], sum_out.at[:, cols], sem.at[1 + n])
            )
            copies[-1].start()
        for copy in copies:
            copy.wait()

    return pl.pallas_call(
        kernel,
        out_shape=[
            jax.ShapeDtypeStruct((tok_count, width), BF16),
            jax.ShapeDtypeStruct(block.shape, block.dtype),
        ],
        in_specs=[VMEM, VMEM, VMEM, HBM],
        out_specs=[HBM, HBM],
        scratch_shapes=[
            pltpu.VMEM((tok_count, width), BF16),
            pltpu.SemaphoreType.DMA((1 + width // chunk,)),
        ],
        input_output_aliases={3: 1},
        compiler_params=pltpu.CompilerParams(vmem_limit_bytes=4 * MIB),
        cost_estimate=pl.CostEstimate(
            flops=2 * slots * tok_count * width,
            bytes_accessed=2 * tok_count * width + block.size,
            transcendentals=0,
        ),
        name="combine",
    )(picker, returned, block, written)


def per_device(
    tokens, grad_out, routing, gates, modality, hot_experts, gate_weight, up_weight, down_weight
):
    def swap(block):
        return lax.ppermute(block, "dp", [(0, 1), (1, 0)])

    def travel(block, hop):
        moves = [
            (2 * i + c, 2 * (i ^ hop ^ c) + c) for i in range(FLIGHT) for c in range(2)
        ]
        return lax.ppermute(block, ("expert", "dp"), moves)

    picker, keep, give, my_tokens, my_grads = route(
        hot_experts, routing, gates, modality, tokens, grad_out
    )
    msgs = pick(keep, swap(give), my_tokens, swap(tokens), my_grads, swap(grad_out))
    got = [travel(m, hop) for m, hop in zip(msgs, HOPS)]
    halves = load_weights(gate_weight, up_weight, down_weight)
    got, halves = lax.optimization_barrier((got, halves))
    own = jnp.concatenate(got, axis=0)
    blocks = [own, swap(own)]
    tok, scl, dh, du, act, mine, theirs = activation_grads(blocks, *halves)
    down_block = weight_grad(scl, act, "down_grad")
    added, down_block = lax.optimization_barrier((swap(theirs), down_block))
    pieces = (mine + added.astype(F32)).astype(BF16)
    back = [
        travel(pieces[2 * k * HOTCAP : 2 * (k + 1) * HOTCAP], hop) for k, hop in enumerate(HOPS)
    ]
    grad_gate, grad_down, up_block = gate_up_grads(tok, dh, du, down_block)
    back, up_block = lax.optimization_barrier((back[::-1], up_block))
    back = back[::-1]
    kept = jnp.concatenate([block[:HOTCAP] for block in back], axis=0)
    given = swap(jnp.concatenate([block[HOTCAP:] for block in back], axis=0))
    given, written = lax.optimization_barrier((given, write_first(up_block)))
    returned = jnp.concatenate([kept, given], axis=0)
    grad_tokens, grad_up = combine(picker, returned, up_block, written)
    return grad_tokens, grad_gate, grad_up, grad_down


def solution(mesh):
    sizes = dict(mesh.shape)
    token_spec = P(("groups", "expert", "dp"), None)
    in_specs = (
        token_spec,
        token_spec,
        token_spec,
        token_spec,
        P(("groups", "expert", "dp")),
        P("groups"),
        P("expert", None),
        P("expert", None),
        P("expert", None),
    )
    paired = sizes["expert"] == FLIGHT and sizes["dp"] == 2
    return jax.shard_map(
        per_device if paired else per_device_general,
        mesh=mesh,
        in_specs=in_specs,
        out_specs=(token_spec,) * 4,
        check_vma=False,
    )
```

```python
import jax
import jax.numpy as jnp
from jax import lax
from jax.experimental import pallas as pl
from jax.experimental.pallas import tpu as pltpu
from jax.sharding import PartitionSpec as P

FLIGHT = 8
HOTCAP = 8
F32 = jnp.float32
BF16 = jnp.bfloat16
MIB = 1 << 20


def expert_pass(in_tokens, in_scaled, gate_rows, up_rows, down_rows):
    pre_gate = jnp.einsum("nd,hd->nh", in_tokens, gate_rows, preferred_element_type=jnp.float32)
    pre_up = jnp.einsum("nd,hd->nh", in_tokens, up_rows, preferred_element_type=jnp.float32)
    sigmoid_gate = jax.nn.sigmoid(pre_gate)
    swish_gate = pre_gate * sigmoid_gate
    activated = (swish_gate * pre_up).astype(jnp.bfloat16)
    grad_act = jnp.einsum("nd,hd->nh", in_scaled, down_rows, preferred_element_type=jnp.float32)
    grad_pre_gate = (
        grad_act * pre_up * sigmoid_gate * (1.0 + pre_gate * (1.0 - sigmoid_gate))
    ).astype(jnp.bfloat16)
    grad_pre_up = (grad_act * swish_gate).astype(jnp.bfloat16)
    gate_term = jnp.einsum(
        "nh,nd->hd", grad_pre_gate, in_tokens, preferred_element_type=jnp.float32
    )
    up_term = jnp.einsum("nh,nd->hd", grad_pre_up, in_tokens, preferred_element_type=jnp.float32)
    down_term = jnp.einsum("nh,nd->hd", activated, in_scaled, preferred_element_type=jnp.float32)
    partials = jnp.dot(grad_pre_gate, gate_rows, preferred_element_type=jnp.float32)
    partials = (
        partials + jnp.dot(grad_pre_up, up_rows, preferred_element_type=jnp.float32)
    ).astype(jnp.bfloat16)
    return (partials, (gate_term, up_term, down_term))


def per_device_general(
    tokens, grad_out, routing, gates, modality, hot_experts, gate_weight, up_weight, down_weight
):
    tok_count, model_width = tokens.shape
    top_count = routing.shape[1]
    hot_count = hot_experts.shape[0]
    devices = lax.axis_size("expert")
    split_count = devices // FLIGHT
    position = lax.broadcasted_iota(jnp.int32, (tok_count, top_count), 1)
    pinned_slot = position - (top_count - hot_count)
    pick_table = pinned_slot[:, :, None] == jnp.arange(hot_count, dtype=jnp.int32)[None, None, :]
    hot_pick = jnp.sum(jnp.where(pick_table, hot_experts[None, None, :], 0), axis=2)
    pinned = (modality[:, None] == 1) & (pinned_slot >= 0)
    chosen = jnp.where(pinned, hot_pick, routing)
    matches = chosen[:, :, None] == jnp.arange(FLIGHT, dtype=jnp.int32)[None, None, :]
    expert_gate = jnp.sum(jnp.where(matches, gates[:, :, None], 0.0), axis=1)
    present = jnp.any(matches, axis=1)
    placed = jnp.cumsum(present.astype(jnp.int32), axis=0) - 1
    slot_ids = jnp.arange(HOTCAP, dtype=jnp.int32)
    chooser = (placed.T[:, None, :] == slot_ids[None, :, None]) & present.T[:, None, :]
    picker = chooser.astype(jnp.bfloat16)
    picked = jnp.einsum("scr,rd->scd", picker, tokens, preferred_element_type=jnp.float32).astype(
        jnp.bfloat16
    )
    picked_grad = jnp.einsum("scr,rd->scd", picker, grad_out, preferred_element_type=jnp.float32)
    slot_gate = jnp.sum(jnp.where(chooser, expert_gate.T[:, None, :], 0.0), axis=2)
    scaled = (picked_grad * slot_gate[:, :, None]).astype(jnp.bfloat16)
    send_shape = (devices, HOTCAP, model_width)

    def replicate_rows(block_data):
        widened = jnp.broadcast_to(block_data[:, None], (FLIGHT, split_count, HOTCAP, model_width))
        return widened.reshape(send_shape)

    got_tokens, got_scaled = (
        lax.all_to_all(replicate_rows(picked), "expert", split_axis=0, concat_axis=0, tiled=True),
        lax.all_to_all(replicate_rows(scaled), "expert", split_axis=0, concat_axis=0, tiled=True),
    )
    partials, grad_terms = expert_pass(
        got_tokens.reshape(-1, model_width),
        got_scaled.reshape(-1, model_width),
        gate_weight,
        up_weight,
        down_weight,
    )
    returned = lax.all_to_all(
        partials.reshape(send_shape), "expert", split_axis=0, concat_axis=0, tiled=True
    )
    returned = returned.reshape(FLIGHT, split_count, HOTCAP, model_width)
    grad_tokens = jnp.einsum(
        "fcr,fpcd->rd", chooser.astype(jnp.bfloat16), returned, preferred_element_type=jnp.float32
    )
    summed = tuple(
        lax.psum_scatter(term, "dp", scatter_dimension=0, tiled=True) for term in grad_terms
    )
    return (grad_tokens.astype(jnp.bfloat16),) + tuple(term.astype(jnp.bfloat16) for term in summed)


HOPS = (7, 4, 2, 1)
CARRIED = len(HOPS) * HOTCAP
NT = (((1,), (1,)), ((), ()))
SMEM = pl.BlockSpec(memory_space=pltpu.SMEM)
VMEM = pl.BlockSpec(memory_space=pltpu.VMEM)
HBM = pl.BlockSpec(memory_space=pltpu.HBM)


def route(hot_experts, routing, gates, modality):
    tok_count, top_count = routing.shape
    hot_count = hot_experts.shape[0]
    slots = FLIGHT * HOTCAP
    hops = len(HOPS)

    def kernel(hot_ref, route_ref, gate_ref, mod_ref, choose_ref, keep_ref, give_ref):
        position = lax.broadcasted_iota(jnp.int32, (top_count, tok_count), 0)
        hot_pick = jnp.zeros((top_count, tok_count), jnp.int32)
        for j in range(hot_count):
            hot_pick = jnp.where(position == top_count - hot_count + j, hot_ref[j], hot_pick)
        pinned = (mod_ref[...] == 1) & (position >= top_count - hot_count)
        chosen = jnp.where(pinned, hot_pick, route_ref[...])
        index = lax.broadcasted_iota(jnp.int32, (FLIGHT, top_count, tok_count), 0)
        hop = jnp.zeros_like(index)
        for k, value in enumerate(HOPS):
            hop = jnp.where(index % hops == k, value, hop)
        expert = hop ^ (index // hops) ^ lax.axis_index("expert") ^ lax.axis_index("dp")
        matches = chosen[None] == expert
        expert_gate = jnp.sum(jnp.where(matches, gate_ref[...][None], 0.0), axis=1)
        present = jnp.sum(jnp.where(matches, 1.0, 0.0), axis=1)
        before = lax.broadcasted_iota(jnp.int32, (tok_count, tok_count), 0)
        after = lax.broadcasted_iota(jnp.int32, (tok_count, tok_count), 1)
        upto = jnp.where(before <= after, 1.0, 0.0).astype(BF16)
        placed = jnp.dot(present.astype(BF16), upto, preferred_element_type=F32)
        slot = lax.broadcasted_iota(jnp.int32, (FLIGHT, HOTCAP, tok_count), 1) + 1
        slot_hit = placed[:, None, :].astype(jnp.int32) == slot
        chooser = slot_hit & (present[:, None, :] > 0.0)
        picker = jnp.where(chooser, 1.0, 0.0).reshape(slots, tok_count)
        gated = jnp.where(chooser, expert_gate[:, None, :], 0.0).reshape(slots, tok_count)
        choose_ref[...] = picker.astype(BF16)
        keep_ref[...] = gated[:CARRIED]
        give_ref[...] = gated[CARRIED:]

    return pl.pallas_call(
        kernel,
        out_shape=[
            pltpu.VMEM((slots, tok_count), BF16),
            pltpu.VMEM((CARRIED, tok_count), F32),
            pltpu.VMEM((slots - CARRIED, tok_count), F32),
        ],
        in_specs=[SMEM, VMEM, VMEM, VMEM],
        out_specs=[VMEM] * 3,
        name="route",
    )(hot_experts, routing.T, gates.T, modality[None, :])


def load_rows(*arrays):
    count = len(arrays)

    def kernel(*refs):
        loads = [
            pltpu.make_async_copy(refs[i], refs[count + i], refs[2 * count].at[i])
            for i in range(count)
        ]
        for load in loads:
            load.start()
        for load in loads:
            load.wait()

    return pl.pallas_call(
        kernel,
        out_shape=[pltpu.VMEM(array.shape, array.dtype) for array in arrays],
        in_specs=[HBM] * count,
        out_specs=[VMEM] * count,
        scratch_shapes=[pltpu.SemaphoreType.DMA((count,))],
        compiler_params=pltpu.CompilerParams(vmem_limit_bytes=2 * MIB),
        cost_estimate=pl.CostEstimate(
            flops=0, bytes_accessed=4 * sum(array.size for array in arrays), transcendentals=0
        ),
        name="load_rows",
    )(*(pltpu.with_memory_space_constraint(array, pltpu.HBM) for array in arrays))


def pick(mine, theirs, my_tokens, their_tokens, my_grads, their_grads):
    tok_count, width = my_tokens.shape

    def kernel(mine_ref, theirs_ref, my_tok, their_tok, my_grad, their_grad, *outs):
        for core, slot_ref, tok_ref, grad_ref in (
            (0, mine_ref, my_tok, my_grad),
            (1, theirs_ref, their_tok, their_grad),
        ):
            gated = slot_ref[...]
            picker = jnp.where(gated != 0.0, 1.0, 0.0).astype(BF16)
            rows = jnp.dot(picker, tok_ref[...], preferred_element_type=F32)
            scaled = jnp.dot(picker, grad_ref[...], preferred_element_type=F32)
            scaled = scaled * jnp.sum(gated, axis=1, keepdims=True)
            for k, out in enumerate(outs):
                slot = slice(k * HOTCAP, (k + 1) * HOTCAP)
                out[core * HOTCAP : (core + 1) * HOTCAP] = rows[slot].astype(BF16)
                out[(core + 2) * HOTCAP : (core + 3) * HOTCAP] = scaled[slot].astype(BF16)

    return pl.pallas_call(
        kernel,
        out_shape=[pltpu.VMEM((4 * HOTCAP, width), BF16)] * len(HOPS),
        in_specs=[VMEM] * 6,
        out_specs=[VMEM] * len(HOPS),
        compiler_params=pltpu.CompilerParams(vmem_limit_bytes=16 * MIB),
        cost_estimate=pl.CostEstimate(
            flops=8 * CARRIED * tok_count * width,
            bytes_accessed=8 * (CARRIED + tok_count) * width,
            transcendentals=0,
        ),
        name="pick",
    )(mine, theirs, my_tokens, their_tokens, my_grads, their_grads)


def load_weights(gate_weight, up_weight, down_weight):
    half = gate_weight.shape[0] // 2
    width = gate_weight.shape[1]
    tile = min(256, half)
    steps = half // tile

    def kernel(g_in, u_in, w_in, g_ref, u_ref, g_cols, u_cols, w_cols, w_ref, sem):
        first = pl.multiple_of(lax.axis_index("dp") * half, half)
        lanes = ((g_in, g_ref, g_cols), (u_in, u_ref, u_cols), (w_in, w_ref, w_cols))
        order = [(lane, i) for lane in range(3) for i in range(steps)]

        def load(lane, i):
            source, target, _ = lanes[lane]
            return pltpu.make_async_copy(
                source.at[pl.ds(first + i * tile, tile)],
                target.at[pl.ds(i * tile, tile)],
                sem.at[lane, i],
            )

        depth = 3
        for step in order[:depth]:
            load(*step).start()
        for n, (lane, i) in enumerate(order):
            load(lane, i).wait()
            if n + depth < len(order):
                load(*order[n + depth]).start()
            _, target, columns = lanes[lane]
            columns[:, i * tile : (i + 1) * tile] = target[i * tile : (i + 1) * tile].T

    return pl.pallas_call(
        kernel,
        out_shape=[pltpu.VMEM((half, width), BF16)] * 2
        + [pltpu.VMEM((width, half), BF16)] * 3,
        in_specs=[HBM] * 3,
        out_specs=[VMEM] * 5,
        scratch_shapes=[pltpu.VMEM((half, width), BF16), pltpu.SemaphoreType.DMA((3, steps))],
        compiler_params=pltpu.CompilerParams(vmem_limit_bytes=10 * MIB),
        cost_estimate=pl.CostEstimate(
            flops=0, bytes_accessed=12 * half * width, transcendentals=0
        ),
        name="load_weights",
    )(
        *(
            pltpu.with_memory_space_constraint(weight, pltpu.HBM)
            for weight in (gate_weight, up_weight, down_weight)
        )
    )


def activation_grads(blocks, gate_half, up_half, gate_cols, up_cols, down_cols):
    width = blocks[0].shape[1]
    rows = 2 * HOTCAP * len(HOPS)
    half = gate_half.shape[0]
    tile = min(256, half)
    chunk = 512 if width % 512 == 0 else width

    def kernel(*refs):
        ins, refs = refs[: len(blocks)], refs[len(blocks) :]
        g_ref, u_ref, g_cols, u_cols, w_cols, tok_ref, scl_ref = refs[:7]
        dh_ref, du_ref, act_ref, mine_ref, theirs_ref, dh_rows, du_rows = refs[7:]
        message = 2 * HOTCAP
        place = 0
        for block in ins:
            for start in range(0, block.shape[0], 2 * message):
                tok_ref[place : place + message] = block[start : start + message]
                scl_ref[place : place + message] = block[start + message : start + 2 * message]
                place += message
        for i in range(half // tile):
            part = slice(i * tile, (i + 1) * tile)
            pre = jnp.dot(tok_ref[...], g_cols[:, part], preferred_element_type=F32)
            up = jnp.dot(tok_ref[...], u_cols[:, part], preferred_element_type=F32)
            da = jnp.dot(scl_ref[...], w_cols[:, part], preferred_element_type=F32)
            sig = jax.nn.sigmoid(pre)
            swish = pre * sig
            act_ref[part] = (swish * up).astype(BF16).T
            dh = (da * up * sig * (1.0 + pre * (1.0 - sig))).astype(BF16)
            du = (da * swish).astype(BF16)
            dh_ref[part] = dh.T
            du_ref[part] = du.T
            dh_rows[:, part] = dh
            du_rows[:, part] = du
        for c in range(0, width, chunk):
            cols = slice(c, c + chunk)
            piece = jnp.dot(dh_rows[...], g_ref[:, cols], preferred_element_type=F32)
            piece += jnp.dot(du_rows[...], u_ref[:, cols], preferred_element_type=F32)
            mine_ref[:, cols] = piece[:rows]
            theirs_ref[:, cols] = piece[rows:].astype(BF16)

    return pl.pallas_call(
        kernel,
        out_shape=[pltpu.VMEM((2 * rows, width), BF16)] * 2
        + [pltpu.VMEM((half, 2 * rows), BF16)] * 3
        + [pltpu.VMEM((rows, width), F32), pltpu.VMEM((rows, width), BF16)],
        in_specs=[VMEM] * (len(blocks) + 5),
        out_specs=[VMEM] * 7,
        scratch_shapes=[pltpu.VMEM((2 * rows, half), BF16)] * 2,
        compiler_params=pltpu.CompilerParams(vmem_limit_bytes=8 * MIB),
        cost_estimate=pl.CostEstimate(
            flops=20 * rows * half * width,
            bytes_accessed=6 * half * width,
            transcendentals=2 * rows * half,
        ),
        name="activation_grads",
    )(*blocks, gate_half, up_half, gate_cols, up_cols, down_cols)


def weight_grad(rows, left, name):
    count, width = rows.shape
    half = left.shape[0]
    chunk = 512 if width % 512 == 0 else width

    def kernel(rows_ref, left_ref, out_ref):
        for c in range(0, width, chunk):
            cols = slice(c, c + chunk)
            out_ref[:, cols] = jnp.dot(
                left_ref[...], rows_ref[:, cols], preferred_element_type=F32
            ).astype(BF16)

    return pl.pallas_call(
        kernel,
        out_shape=pltpu.VMEM((half, width), BF16),
        in_specs=[VMEM, VMEM],
        out_specs=VMEM,
        compiler_params=pltpu.CompilerParams(vmem_limit_bytes=8 * MIB),
        cost_estimate=pl.CostEstimate(
            flops=2 * count * half * width, bytes_accessed=2 * half * width, transcendentals=0
        ),
        name=name,
    )(rows, left)


def gate_up_grads(rows, gate_left, up_left, down):
    count, width = rows.shape
    half = gate_left.shape[0]
    chunk = 512 if width % 512 == 0 else width

    def kernel(rows_ref, gate_ref, up_ref, down_ref, gate_out, down_out, up_out, held, sem):
        copies = [pltpu.make_async_copy(down_ref, down_out, sem.at[0])]
        copies[0].start()
        for n, c in enumerate(range(0, width, chunk)):
            cols = slice(c, c + chunk)
            held[:, cols] = jnp.dot(
                gate_ref[...], rows_ref[:, cols], preferred_element_type=F32
            ).astype(BF16)
            copies.append(
                pltpu.make_async_copy(held.at[:, cols], gate_out.at[:, cols], sem.at[1 + n])
            )
            copies[-1].start()
        for c in range(0, width, chunk):
            cols = slice(c, c + chunk)
            up_out[:, cols] = jnp.dot(
                up_ref[...], rows_ref[:, cols], preferred_element_type=F32
            ).astype(BF16)
        for copy in copies:
            copy.wait()

    full = jax.ShapeDtypeStruct((half, width), BF16)
    return pl.pallas_call(
        kernel,
        out_shape=[full, full, pltpu.VMEM((half, width), BF16)],
        in_specs=[VMEM] * 4,
        out_specs=[HBM, HBM, VMEM],
        scratch_shapes=[
            pltpu.VMEM((half, width), BF16),
            pltpu.SemaphoreType.DMA((1 + width // chunk,)),
        ],
        compiler_params=pltpu.CompilerParams(vmem_limit_bytes=12 * MIB),
        cost_estimate=pl.CostEstimate(
            flops=4 * count * half * width, bytes_accessed=4 * half * width, transcendentals=0
        ),
        name="gate_up_grads",
    )(rows, gate_left, up_left, down)


def write_first(block):
    rows = block.shape[0] // 2

    def kernel(block_ref, out, sem):
        copy = pltpu.make_async_copy(block_ref.at[pl.ds(0, rows)], out.at[pl.ds(0, rows)], sem)
        copy.start()
        copy.wait()

    return pl.pallas_call(
        kernel,
        out_shape=jax.ShapeDtypeStruct(block.shape, block.dtype),
        in_specs=[VMEM],
        out_specs=HBM,
        scratch_shapes=[pltpu.SemaphoreType.DMA],
        compiler_params=pltpu.CompilerParams(vmem_limit_bytes=2 * MIB),
        cost_estimate=pl.CostEstimate(
            flops=0, bytes_accessed=2 * block.size, transcendentals=0
        ),
        name="write_first",
    )(block)


def combine(picker, returned, block, written):
    slots, tok_count = picker.shape
    width = returned.shape[1]
    rows = block.shape[0] // 2
    chunk = 512 if width % 512 == 0 else width

    def kernel(pick_ref, back_ref, block_ref, _, sum_out, block_out, held, sem):
        rest = pl.ds(rows, rows)
        copies = [pltpu.make_async_copy(block_ref.at[rest], block_out.at[rest], sem.at[0])]
        copies[0].start()
        chooser = pick_ref[...].T
        for n, c in enumerate(range(0, width, chunk)):
            cols = slice(c, c + chunk)
            held[:, cols] = jnp.dot(
                chooser, back_ref[:, cols], preferred_element_type=F32
            ).astype(BF16)
            copies.append(
                pltpu.make_async_copy(held.at[:, cols], sum_out.at[:, cols], sem.at[1 + n])
            )
            copies[-1].start()
        for copy in copies:
            copy.wait()

    return pl.pallas_call(
        kernel,
        out_shape=[
            jax.ShapeDtypeStruct((tok_count, width), BF16),
            jax.ShapeDtypeStruct(block.shape, block.dtype),
        ],
        in_specs=[VMEM, VMEM, VMEM, HBM],
        out_specs=[HBM, HBM],
        scratch_shapes=[
            pltpu.VMEM((tok_count, width), BF16),
            pltpu.SemaphoreType.DMA((1 + width // chunk,)),
        ],
        input_output_aliases={3: 1},
        compiler_params=pltpu.CompilerParams(vmem_limit_bytes=4 * MIB),
        cost_estimate=pl.CostEstimate(
            flops=2 * slots * tok_count * width,
            bytes_accessed=2 * tok_count * width + block.size,
            transcendentals=0,
        ),
        name="combine",
    )(picker, returned, block, written)


def per_device(
    tokens, grad_out, routing, gates, modality, hot_experts, gate_weight, up_weight, down_weight
):
    def swap(block):
        return lax.ppermute(block, "dp", [(0, 1), (1, 0)])

    def travel(block, hop):
        moves = [
            (2 * i + c, 2 * (i ^ hop ^ c) + c) for i in range(FLIGHT) for c in range(2)
        ]
        return lax.ppermute(block, ("expert", "dp"), moves)

    picker, keep, give = route(hot_experts, routing, gates, modality)
    my_tokens, my_grads = load_rows(tokens, grad_out)
    msgs = pick(keep, swap(give), my_tokens, swap(tokens), my_grads, swap(grad_out))
    got = [travel(m, hop) for m, hop in zip(msgs, HOPS)]
    halves = load_weights(gate_weight, up_weight, down_weight)
    got, halves = lax.optimization_barrier((got, halves))
    own = jnp.concatenate(got, axis=0)
    blocks = [own, swap(own)]
    tok, scl, dh, du, act, mine, theirs = activation_grads(blocks, *halves)
    down_block = weight_grad(scl, act, "down_grad")
    added, down_block = lax.optimization_barrier((swap(theirs), down_block))
    pieces = (mine + added.astype(F32)).astype(BF16)
    back = [
        travel(pieces[2 * k * HOTCAP : 2 * (k + 1) * HOTCAP], hop) for k, hop in enumerate(HOPS)
    ]
    grad_gate, grad_down, up_block = gate_up_grads(tok, dh, du, down_block)
    back, up_block = lax.optimization_barrier((back[::-1], up_block))
    back = back[::-1]
    kept = jnp.concatenate([block[:HOTCAP] for block in back], axis=0)
    given = swap(jnp.concatenate([block[HOTCAP:] for block in back], axis=0))
    given, written = lax.optimization_barrier((given, write_first(up_block)))
    returned = jnp.concatenate([kept, given], axis=0)
    grad_tokens, grad_up = combine(picker, returned, up_block, written)
    return grad_tokens, grad_gate, grad_up, grad_down


def solution(mesh):
    sizes = dict(mesh.shape)
    token_spec = P(("groups", "expert", "dp"), None)
    in_specs = (
        token_spec,
        token_spec,
        token_spec,
        token_spec,
        P(("groups", "expert", "dp")),
        P("groups"),
        P("expert", None),
        P("expert", None),
        P("expert", None),
    )
    paired = sizes["expert"] == FLIGHT and sizes["dp"] == 2
    return jax.shard_map(
        per_device if paired else per_device_general,
        mesh=mesh,
        in_specs=in_specs,
        out_specs=(token_spec,) * 4,
        check_vma=False,
    )
```

```python
import jax
import jax.numpy as jnp
from jax import lax
from jax.experimental import pallas as pl
from jax.experimental.pallas import tpu as pltpu
from jax.sharding import PartitionSpec as P

FLIGHT = 8
HOTCAP = 8
F32 = jnp.float32
BF16 = jnp.bfloat16
MIB = 1 << 20


def expert_pass(in_tokens, in_scaled, gate_rows, up_rows, down_rows):
    pre_gate = jnp.einsum("nd,hd->nh", in_tokens, gate_rows, preferred_element_type=jnp.float32)
    pre_up = jnp.einsum("nd,hd->nh", in_tokens, up_rows, preferred_element_type=jnp.float32)
    sigmoid_gate = jax.nn.sigmoid(pre_gate)
    swish_gate = pre_gate * sigmoid_gate
    activated = (swish_gate * pre_up).astype(jnp.bfloat16)
    grad_act = jnp.einsum("nd,hd->nh", in_scaled, down_rows, preferred_element_type=jnp.float32)
    grad_pre_gate = (
        grad_act * pre_up * sigmoid_gate * (1.0 + pre_gate * (1.0 - sigmoid_gate))
    ).astype(jnp.bfloat16)
    grad_pre_up = (grad_act * swish_gate).astype(jnp.bfloat16)
    gate_term = jnp.einsum(
        "nh,nd->hd", grad_pre_gate, in_tokens, preferred_element_type=jnp.float32
    )
    up_term = jnp.einsum("nh,nd->hd", grad_pre_up, in_tokens, preferred_element_type=jnp.float32)
    down_term = jnp.einsum("nh,nd->hd", activated, in_scaled, preferred_element_type=jnp.float32)
    partials = jnp.dot(grad_pre_gate, gate_rows, preferred_element_type=jnp.float32)
    partials = (
        partials + jnp.dot(grad_pre_up, up_rows, preferred_element_type=jnp.float32)
    ).astype(jnp.bfloat16)
    return (partials, (gate_term, up_term, down_term))


def per_device_general(
    tokens, grad_out, routing, gates, modality, hot_experts, gate_weight, up_weight, down_weight
):
    tok_count, model_width = tokens.shape
    top_count = routing.shape[1]
    hot_count = hot_experts.shape[0]
    devices = lax.axis_size("expert")
    split_count = devices // FLIGHT
    position = lax.broadcasted_iota(jnp.int32, (tok_count, top_count), 1)
    pinned_slot = position - (top_count - hot_count)
    pick_table = pinned_slot[:, :, None] == jnp.arange(hot_count, dtype=jnp.int32)[None, None, :]
    hot_pick = jnp.sum(jnp.where(pick_table, hot_experts[None, None, :], 0), axis=2)
    pinned = (modality[:, None] == 1) & (pinned_slot >= 0)
    chosen = jnp.where(pinned, hot_pick, routing)
    matches = chosen[:, :, None] == jnp.arange(FLIGHT, dtype=jnp.int32)[None, None, :]
    expert_gate = jnp.sum(jnp.where(matches, gates[:, :, None], 0.0), axis=1)
    present = jnp.any(matches, axis=1)
    placed = jnp.cumsum(present.astype(jnp.int32), axis=0) - 1
    slot_ids = jnp.arange(HOTCAP, dtype=jnp.int32)
    chooser = (placed.T[:, None, :] == slot_ids[None, :, None]) & present.T[:, None, :]
    picker = chooser.astype(jnp.bfloat16)
    picked = jnp.einsum("scr,rd->scd", picker, tokens, preferred_element_type=jnp.float32).astype(
        jnp.bfloat16
    )
    picked_grad = jnp.einsum("scr,rd->scd", picker, grad_out, preferred_element_type=jnp.float32)
    slot_gate = jnp.sum(jnp.where(chooser, expert_gate.T[:, None, :], 0.0), axis=2)
    scaled = (picked_grad * slot_gate[:, :, None]).astype(jnp.bfloat16)
    send_shape = (devices, HOTCAP, model_width)

    def replicate_rows(block_data):
        widened = jnp.broadcast_to(block_data[:, None], (FLIGHT, split_count, HOTCAP, model_width))
        return widened.reshape(send_shape)

    got_tokens, got_scaled = (
        lax.all_to_all(replicate_rows(picked), "expert", split_axis=0, concat_axis=0, tiled=True),
        lax.all_to_all(replicate_rows(scaled), "expert", split_axis=0, concat_axis=0, tiled=True),
    )
    partials, grad_terms = expert_pass(
        got_tokens.reshape(-1, model_width),
        got_scaled.reshape(-1, model_width),
        gate_weight,
        up_weight,
        down_weight,
    )
    returned = lax.all_to_all(
        partials.reshape(send_shape), "expert", split_axis=0, concat_axis=0, tiled=True
    )
    returned = returned.reshape(FLIGHT, split_count, HOTCAP, model_width)
    grad_tokens = jnp.einsum(
        "fcr,fpcd->rd", chooser.astype(jnp.bfloat16), returned, preferred_element_type=jnp.float32
    )
    summed = tuple(
        lax.psum_scatter(term, "dp", scatter_dimension=0, tiled=True) for term in grad_terms
    )
    return (grad_tokens.astype(jnp.bfloat16),) + tuple(term.astype(jnp.bfloat16) for term in summed)


HOPS = (7, 4, 2, 1)
CARRIED = len(HOPS) * HOTCAP
NT = (((1,), (1,)), ((), ()))
SMEM = pl.BlockSpec(memory_space=pltpu.SMEM)
VMEM = pl.BlockSpec(memory_space=pltpu.VMEM)
HBM = pl.BlockSpec(memory_space=pltpu.HBM)


def route(hot_experts, routing, gates, modality):
    tok_count, top_count = routing.shape
    hot_count = hot_experts.shape[0]
    slots = FLIGHT * HOTCAP
    hops = len(HOPS)

    def kernel(hot_ref, route_ref, gate_ref, mod_ref, choose_ref, keep_ref, give_ref):
        position = lax.broadcasted_iota(jnp.int32, (top_count, tok_count), 0)
        hot_pick = jnp.zeros((top_count, tok_count), jnp.int32)
        for j in range(hot_count):
            hot_pick = jnp.where(position == top_count - hot_count + j, hot_ref[j], hot_pick)
        pinned = (mod_ref[...] == 1) & (position >= top_count - hot_count)
        chosen = jnp.where(pinned, hot_pick, route_ref[...])
        index = lax.broadcasted_iota(jnp.int32, (FLIGHT, top_count, tok_count), 0)
        hop = jnp.zeros_like(index)
        for k, value in enumerate(HOPS):
            hop = jnp.where(index % hops == k, value, hop)
        expert = hop ^ (index // hops) ^ lax.axis_index("expert") ^ lax.axis_index("dp")
        matches = chosen[None] == expert
        expert_gate = jnp.sum(jnp.where(matches, gate_ref[...][None], 0.0), axis=1)
        present = jnp.sum(jnp.where(matches, 1.0, 0.0), axis=1)
        before = lax.broadcasted_iota(jnp.int32, (tok_count, tok_count), 0)
        after = lax.broadcasted_iota(jnp.int32, (tok_count, tok_count), 1)
        upto = jnp.where(before <= after, 1.0, 0.0).astype(BF16)
        placed = jnp.dot(present.astype(BF16), upto, preferred_element_type=F32)
        slot = lax.broadcasted_iota(jnp.int32, (FLIGHT, HOTCAP, tok_count), 1) + 1
        slot_hit = placed[:, None, :].astype(jnp.int32) == slot
        chooser = slot_hit & (present[:, None, :] > 0.0)
        picker = jnp.where(chooser, 1.0, 0.0).reshape(slots, tok_count)
        gated = jnp.where(chooser, expert_gate[:, None, :], 0.0).reshape(slots, tok_count)
        choose_ref[...] = picker.astype(BF16)
        keep_ref[...] = gated[:CARRIED]
        give_ref[...] = gated[CARRIED:]

    return pl.pallas_call(
        kernel,
        out_shape=[
            pltpu.VMEM((slots, tok_count), BF16),
            pltpu.VMEM((CARRIED, tok_count), F32),
            pltpu.VMEM((slots - CARRIED, tok_count), F32),
        ],
        in_specs=[SMEM, VMEM, VMEM, VMEM],
        out_specs=[VMEM] * 3,
        name="route",
    )(hot_experts, routing.T, gates.T, modality[None, :])


def load_rows(*arrays):
    count = len(arrays)

    def kernel(*refs):
        loads = [
            pltpu.make_async_copy(refs[i], refs[count + i], refs[2 * count].at[i])
            for i in range(count)
        ]
        for load in loads:
            load.start()
        for load in loads:
            load.wait()

    return pl.pallas_call(
        kernel,
        out_shape=[pltpu.VMEM(array.shape, array.dtype) for array in arrays],
        in_specs=[HBM] * count,
        out_specs=[VMEM] * count,
        scratch_shapes=[pltpu.SemaphoreType.DMA((count,))],
        compiler_params=pltpu.CompilerParams(vmem_limit_bytes=2 * MIB),
        cost_estimate=pl.CostEstimate(
            flops=0, bytes_accessed=4 * sum(array.size for array in arrays), transcendentals=0
        ),
        name="load_rows",
    )(*(pltpu.with_memory_space_constraint(array, pltpu.HBM) for array in arrays))


def pick(mine, theirs, my_tokens, their_tokens, my_grads, their_grads):
    tok_count, width = my_tokens.shape

    def kernel(mine_ref, theirs_ref, my_tok, their_tok, my_grad, their_grad, *outs):
        for core, slot_ref, tok_ref, grad_ref in (
            (0, mine_ref, my_tok, my_grad),
            (1, theirs_ref, their_tok, their_grad),
        ):
            gated = slot_ref[...]
            picker = jnp.where(gated != 0.0, 1.0, 0.0).astype(BF16)
            rows = jnp.dot(picker, tok_ref[...], preferred_element_type=F32)
            scaled = jnp.dot(picker, grad_ref[...], preferred_element_type=F32)
            scaled = scaled * jnp.sum(gated, axis=1, keepdims=True)
            for k, out in enumerate(outs):
                slot = slice(k * HOTCAP, (k + 1) * HOTCAP)
                out[core * HOTCAP : (core + 1) * HOTCAP] = rows[slot].astype(BF16)
                out[(core + 2) * HOTCAP : (core + 3) * HOTCAP] = scaled[slot].astype(BF16)

    return pl.pallas_call(
        kernel,
        out_shape=[pltpu.VMEM((4 * HOTCAP, width), BF16)] * len(HOPS),
        in_specs=[VMEM] * 6,
        out_specs=[VMEM] * len(HOPS),
        compiler_params=pltpu.CompilerParams(vmem_limit_bytes=16 * MIB),
        cost_estimate=pl.CostEstimate(
            flops=8 * CARRIED * tok_count * width,
            bytes_accessed=8 * (CARRIED + tok_count) * width,
            transcendentals=0,
        ),
        name="pick",
    )(mine, theirs, my_tokens, their_tokens, my_grads, their_grads)


def load_weights(gate_weight, up_weight, down_weight):
    half = gate_weight.shape[0] // 2
    width = gate_weight.shape[1]
    tile = min(256, half)
    steps = half // tile

    def kernel(g_in, u_in, w_in, g_ref, u_ref, g_cols, u_cols, w_cols, w_ref, sem):
        first = pl.multiple_of(lax.axis_index("dp") * half, half)
        lanes = ((g_in, g_ref, g_cols), (u_in, u_ref, u_cols), (w_in, w_ref, w_cols))
        order = [(lane, i) for lane in range(3) for i in range(steps)]

        def load(lane, i):
            source, target, _ = lanes[lane]
            return pltpu.make_async_copy(
                source.at[pl.ds(first + i * tile, tile)],
                target.at[pl.ds(i * tile, tile)],
                sem.at[lane, i],
            )

        depth = 3
        for step in order[:depth]:
            load(*step).start()
        for n, (lane, i) in enumerate(order):
            load(lane, i).wait()
            if n + depth < len(order):
                load(*order[n + depth]).start()
            _, target, columns = lanes[lane]
            columns[:, i * tile : (i + 1) * tile] = target[i * tile : (i + 1) * tile].T

    return pl.pallas_call(
        kernel,
        out_shape=[pltpu.VMEM((half, width), BF16)] * 2
        + [pltpu.VMEM((width, half), BF16)] * 3,
        in_specs=[HBM] * 3,
        out_specs=[VMEM] * 5,
        scratch_shapes=[pltpu.VMEM((half, width), BF16), pltpu.SemaphoreType.DMA((3, steps))],
        compiler_params=pltpu.CompilerParams(vmem_limit_bytes=10 * MIB),
        cost_estimate=pl.CostEstimate(
            flops=0, bytes_accessed=12 * half * width, transcendentals=0
        ),
        name="load_weights",
    )(
        *(
            pltpu.with_memory_space_constraint(weight, pltpu.HBM)
            for weight in (gate_weight, up_weight, down_weight)
        )
    )


def activation_grads(blocks, gate_half, up_half, gate_cols, up_cols, down_cols):
    width = blocks[0].shape[1]
    rows = 2 * HOTCAP * len(HOPS)
    half = gate_half.shape[0]
    tile = min(256, half)
    chunk = 512 if width % 512 == 0 else width

    def kernel(*refs):
        ins, refs = refs[: len(blocks)], refs[len(blocks) :]
        g_ref, u_ref, g_cols, u_cols, w_cols, tok_ref, scl_ref = refs[:7]
        dh_ref, du_ref, act_ref, mine_ref, theirs_ref, dh_rows, du_rows = refs[7:]
        message = 2 * HOTCAP
        place = 0
        for block in ins:
            for start in range(0, block.shape[0], 2 * message):
                tok_ref[place : place + message] = block[start : start + message]
                scl_ref[place : place + message] = block[start + message : start + 2 * message]
                place += message
        for i in range(half // tile):
            part = slice(i * tile, (i + 1) * tile)
            pre = jnp.dot(tok_ref[...], g_cols[:, part], preferred_element_type=F32)
            up = jnp.dot(tok_ref[...], u_cols[:, part], preferred_element_type=F32)
            da = jnp.dot(scl_ref[...], w_cols[:, part], preferred_element_type=F32)
            sig = jax.nn.sigmoid(pre)
            swish = pre * sig
            act_ref[part] = (swish * up).astype(BF16).T
            dh = (da * up * sig * (1.0 + pre * (1.0 - sig))).astype(BF16)
            du = (da * swish).astype(BF16)
            dh_ref[part] = dh.T
            du_ref[part] = du.T
            dh_rows[:, part] = dh
            du_rows[:, part] = du
        for c in range(0, width, chunk):
            cols = slice(c, c + chunk)
            piece = jnp.dot(dh_rows[...], g_ref[:, cols], preferred_element_type=F32)
            piece += jnp.dot(du_rows[...], u_ref[:, cols], preferred_element_type=F32)
            mine_ref[:, cols] = piece[:rows]
            theirs_ref[:, cols] = piece[rows:].astype(BF16)

    return pl.pallas_call(
        kernel,
        out_shape=[pltpu.VMEM((2 * rows, width), BF16)] * 2
        + [pltpu.VMEM((half, 2 * rows), BF16)] * 3
        + [pltpu.VMEM((rows, width), F32), pltpu.VMEM((rows, width), BF16)],
        in_specs=[VMEM] * (len(blocks) + 5),
        out_specs=[VMEM] * 7,
        scratch_shapes=[pltpu.VMEM((2 * rows, half), BF16)] * 2,
        compiler_params=pltpu.CompilerParams(vmem_limit_bytes=8 * MIB),
        cost_estimate=pl.CostEstimate(
            flops=20 * rows * half * width,
            bytes_accessed=6 * half * width,
            transcendentals=2 * rows * half,
        ),
        name="activation_grads",
    )(*blocks, gate_half, up_half, gate_cols, up_cols, down_cols)


def column_chunks(width):
    chunk = 512 if width % 512 == 0 else width
    return [slice(c, c + chunk) for c in range(0, width, chunk)]


def written_after(chunks):
    return 2 * len(chunks) // 7, 5 * len(chunks) // 7


def down_grads(rows, left):
    count, width = rows.shape
    half = left.shape[0]
    chunks = column_chunks(width)
    early = len(chunks) // 2

    def kernel(rows_ref, left_ref, held, out, sem):
        copies = []
        for n, cols in enumerate(chunks):
            held[:, cols] = jnp.dot(
                left_ref[...], rows_ref[:, cols], preferred_element_type=F32
            ).astype(BF16)
            if n < early:
                copies.append(
                    pltpu.make_async_copy(held.at[:, cols], out.at[:, cols], sem.at[n])
                )
                copies[-1].start()
        for copy in copies:
            copy.wait()

    return pl.pallas_call(
        kernel,
        out_shape=[
            pltpu.VMEM((half, width), BF16),
            jax.ShapeDtypeStruct((half, width), BF16),
        ],
        in_specs=[VMEM, VMEM],
        out_specs=[VMEM, HBM],
        scratch_shapes=[pltpu.SemaphoreType.DMA((len(chunks),))],
        compiler_params=pltpu.CompilerParams(vmem_limit_bytes=8 * MIB),
        cost_estimate=pl.CostEstimate(
            flops=2 * count * half * width, bytes_accessed=2 * half * width, transcendentals=0
        ),
        name="down_grads",
    )(rows, left)


def gate_up_grads(rows, gate_left, up_left, down, down_written):
    count, width = rows.shape
    half = gate_left.shape[0]
    chunks = column_chunks(width)
    early = len(chunks) // 2
    shares = written_after(chunks)

    def kernel(rows_ref, gate_ref, up_ref, down_ref, _, *refs):
        gate_out, down_out, up_held, up_out, held, sem = refs
        copies = []
        for n, cols in enumerate(chunks):
            if n >= early:
                copies.append(
                    pltpu.make_async_copy(down_ref.at[:, cols], down_out.at[:, cols], sem.at[0, n])
                )
                copies[-1].start()
        for n, cols in enumerate(chunks):
            held[:, cols] = jnp.dot(
                gate_ref[...], rows_ref[:, cols], preferred_element_type=F32
            ).astype(BF16)
            copies.append(
                pltpu.make_async_copy(held.at[:, cols], gate_out.at[:, cols], sem.at[1, n])
            )
            copies[-1].start()
        for n, cols in enumerate(chunks):
            up_held[:, cols] = jnp.dot(
                up_ref[...], rows_ref[:, cols], preferred_element_type=F32
            ).astype(BF16)
            if n < shares[0]:
                copies.append(
                    pltpu.make_async_copy(up_held.at[:, cols], up_out.at[:, cols], sem.at[2, n])
                )
                copies[-1].start()
        for copy in copies:
            copy.wait()

    full = jax.ShapeDtypeStruct((half, width), BF16)
    return pl.pallas_call(
        kernel,
        out_shape=[full, full, pltpu.VMEM((half, width), BF16), full],
        in_specs=[VMEM] * 4 + [HBM],
        out_specs=[HBM, HBM, VMEM, HBM],
        scratch_shapes=[
            pltpu.VMEM((half, width), BF16),
            pltpu.SemaphoreType.DMA((3, len(chunks))),
        ],
        input_output_aliases={4: 1},
        compiler_params=pltpu.CompilerParams(vmem_limit_bytes=12 * MIB),
        cost_estimate=pl.CostEstimate(
            flops=4 * count * half * width, bytes_accessed=4 * half * width, transcendentals=0
        ),
        name="gate_up_grads",
    )(rows, gate_left, up_left, down, down_written)


def write_more(block, written):
    chunks = column_chunks(block.shape[1])
    start, stop = written_after(chunks)
    first = chunks[start].start
    cols = pl.ds(first, chunks[stop].start - first)

    def kernel(block_ref, _, out, sem):
        copy = pltpu.make_async_copy(block_ref.at[:, cols], out.at[:, cols], sem)
        copy.start()
        copy.wait()

    return pl.pallas_call(
        kernel,
        out_shape=jax.ShapeDtypeStruct(block.shape, block.dtype),
        in_specs=[VMEM, HBM],
        out_specs=HBM,
        scratch_shapes=[pltpu.SemaphoreType.DMA],
        input_output_aliases={1: 0},
        compiler_params=pltpu.CompilerParams(vmem_limit_bytes=2 * MIB),
        cost_estimate=pl.CostEstimate(
            flops=0, bytes_accessed=2 * block.size, transcendentals=0
        ),
        name="write_more",
    )(block, written)


def combine(picker, returned, block, written):
    slots, tok_count = picker.shape
    width = returned.shape[1]
    chunks = column_chunks(width)
    first = chunks[written_after(chunks)[1]].start

    def kernel(pick_ref, back_ref, block_ref, _, sum_out, block_out, held, sem):
        rest = pl.ds(first, width - first)
        copies = [pltpu.make_async_copy(block_ref.at[:, rest], block_out.at[:, rest], sem.at[0])]
        copies[0].start()
        chooser = pick_ref[...].T
        for n, cols in enumerate(chunks):
            held[:, cols] = jnp.dot(
                chooser, back_ref[:, cols], preferred_element_type=F32
            ).astype(BF16)
            copies.append(
                pltpu.make_async_copy(held.at[:, cols], sum_out.at[:, cols], sem.at[1 + n])
            )
            copies[-1].start()
        for copy in copies:
            copy.wait()

    return pl.pallas_call(
        kernel,
        out_shape=[
            jax.ShapeDtypeStruct((tok_count, width), BF16),
            jax.ShapeDtypeStruct(block.shape, block.dtype),
        ],
        in_specs=[VMEM, VMEM, VMEM, HBM],
        out_specs=[HBM, HBM],
        scratch_shapes=[
            pltpu.VMEM((tok_count, width), BF16),
            pltpu.SemaphoreType.DMA((1 + len(chunks),)),
        ],
        input_output_aliases={3: 1},
        compiler_params=pltpu.CompilerParams(vmem_limit_bytes=4 * MIB),
        cost_estimate=pl.CostEstimate(
            flops=2 * slots * tok_count * width,
            bytes_accessed=2 * tok_count * width + block.size,
            transcendentals=0,
        ),
        name="combine",
    )(picker, returned, block, written)


def per_device(
    tokens, grad_out, routing, gates, modality, hot_experts, gate_weight, up_weight, down_weight
):
    def swap(block):
        return lax.ppermute(block, "dp", [(0, 1), (1, 0)])

    def travel(block, hop):
        moves = [
            (2 * i + c, 2 * (i ^ hop ^ c) + c) for i in range(FLIGHT) for c in range(2)
        ]
        return lax.ppermute(block, ("expert", "dp"), moves)

    picker, keep, give = route(hot_experts, routing, gates, modality)
    my_tokens, my_grads = load_rows(tokens, grad_out)
    msgs = pick(keep, swap(give), my_tokens, swap(tokens), my_grads, swap(grad_out))
    got = [travel(m, hop) for m, hop in zip(msgs, HOPS)]
    halves = load_weights(gate_weight, up_weight, down_weight)
    got, halves = lax.optimization_barrier((got, halves))
    own = jnp.concatenate(got, axis=0)
    blocks = [own, swap(own)]
    tok, scl, dh, du, act, mine, theirs = activation_grads(blocks, *halves)
    down = down_grads(scl, act)
    added, down = lax.optimization_barrier((swap(theirs), down))
    pieces = (mine + added.astype(F32)).astype(BF16)
    back = [
        travel(pieces[2 * k * HOTCAP : 2 * (k + 1) * HOTCAP], hop) for k, hop in enumerate(HOPS)
    ]
    grad_gate, grad_down, up_block, written = gate_up_grads(tok, dh, du, *down)
    back, up_block = lax.optimization_barrier((back[::-1], up_block))
    back = back[::-1]
    kept = jnp.concatenate([block[:HOTCAP] for block in back], axis=0)
    given = swap(jnp.concatenate([block[HOTCAP:] for block in back], axis=0))
    given, written = lax.optimization_barrier((given, write_more(up_block, written)))
    returned = jnp.concatenate([kept, given], axis=0)
    grad_tokens, grad_up = combine(picker, returned, up_block, written)
    return grad_tokens, grad_gate, grad_up, grad_down


def solution(mesh):
    sizes = dict(mesh.shape)
    token_spec = P(("groups", "expert", "dp"), None)
    in_specs = (
        token_spec,
        token_spec,
        token_spec,
        token_spec,
        P(("groups", "expert", "dp")),
        P("groups"),
        P("expert", None),
        P("expert", None),
        P("expert", None),
    )
    paired = sizes["expert"] == FLIGHT and sizes["dp"] == 2
    return jax.shard_map(
        per_device if paired else per_device_general,
        mesh=mesh,
        in_specs=in_specs,
        out_specs=(token_spec,) * 4,
        check_vma=False,
    )
```

```python
import jax
import jax.numpy as jnp
from jax import lax
from jax.experimental import pallas as pl
from jax.experimental.pallas import tpu as pltpu
from jax.sharding import PartitionSpec as P

FLIGHT = 8
HOTCAP = 8
F32 = jnp.float32
BF16 = jnp.bfloat16
MIB = 1 << 20


def expert_pass(in_tokens, in_scaled, gate_rows, up_rows, down_rows):
    pre_gate = jnp.einsum("nd,hd->nh", in_tokens, gate_rows, preferred_element_type=jnp.float32)
    pre_up = jnp.einsum("nd,hd->nh", in_tokens, up_rows, preferred_element_type=jnp.float32)
    sigmoid_gate = jax.nn.sigmoid(pre_gate)
    swish_gate = pre_gate * sigmoid_gate
    activated = (swish_gate * pre_up).astype(jnp.bfloat16)
    grad_act = jnp.einsum("nd,hd->nh", in_scaled, down_rows, preferred_element_type=jnp.float32)
    grad_pre_gate = (
        grad_act * pre_up * sigmoid_gate * (1.0 + pre_gate * (1.0 - sigmoid_gate))
    ).astype(jnp.bfloat16)
    grad_pre_up = (grad_act * swish_gate).astype(jnp.bfloat16)
    gate_term = jnp.einsum(
        "nh,nd->hd", grad_pre_gate, in_tokens, preferred_element_type=jnp.float32
    )
    up_term = jnp.einsum("nh,nd->hd", grad_pre_up, in_tokens, preferred_element_type=jnp.float32)
    down_term = jnp.einsum("nh,nd->hd", activated, in_scaled, preferred_element_type=jnp.float32)
    partials = jnp.dot(grad_pre_gate, gate_rows, preferred_element_type=jnp.float32)
    partials = (
        partials + jnp.dot(grad_pre_up, up_rows, preferred_element_type=jnp.float32)
    ).astype(jnp.bfloat16)
    return (partials, (gate_term, up_term, down_term))


def per_device_general(
    tokens, grad_out, routing, gates, modality, hot_experts, gate_weight, up_weight, down_weight
):
    tok_count, model_width = tokens.shape
    top_count = routing.shape[1]
    hot_count = hot_experts.shape[0]
    devices = lax.axis_size("expert")
    split_count = devices // FLIGHT
    position = lax.broadcasted_iota(jnp.int32, (tok_count, top_count), 1)
    pinned_slot = position - (top_count - hot_count)
    pick_table = pinned_slot[:, :, None] == jnp.arange(hot_count, dtype=jnp.int32)[None, None, :]
    hot_pick = jnp.sum(jnp.where(pick_table, hot_experts[None, None, :], 0), axis=2)
    pinned = (modality[:, None] == 1) & (pinned_slot >= 0)
    chosen = jnp.where(pinned, hot_pick, routing)
    matches = chosen[:, :, None] == jnp.arange(FLIGHT, dtype=jnp.int32)[None, None, :]
    expert_gate = jnp.sum(jnp.where(matches, gates[:, :, None], 0.0), axis=1)
    present = jnp.any(matches, axis=1)
    placed = jnp.cumsum(present.astype(jnp.int32), axis=0) - 1
    slot_ids = jnp.arange(HOTCAP, dtype=jnp.int32)
    chooser = (placed.T[:, None, :] == slot_ids[None, :, None]) & present.T[:, None, :]
    picker = chooser.astype(jnp.bfloat16)
    picked = jnp.einsum("scr,rd->scd", picker, tokens, preferred_element_type=jnp.float32).astype(
        jnp.bfloat16
    )
    picked_grad = jnp.einsum("scr,rd->scd", picker, grad_out, preferred_element_type=jnp.float32)
    slot_gate = jnp.sum(jnp.where(chooser, expert_gate.T[:, None, :], 0.0), axis=2)
    scaled = (picked_grad * slot_gate[:, :, None]).astype(jnp.bfloat16)
    send_shape = (devices, HOTCAP, model_width)

    def replicate_rows(block_data):
        widened = jnp.broadcast_to(block_data[:, None], (FLIGHT, split_count, HOTCAP, model_width))
        return widened.reshape(send_shape)

    got_tokens, got_scaled = (
        lax.all_to_all(replicate_rows(picked), "expert", split_axis=0, concat_axis=0, tiled=True),
        lax.all_to_all(replicate_rows(scaled), "expert", split_axis=0, concat_axis=0, tiled=True),
    )
    partials, grad_terms = expert_pass(
        got_tokens.reshape(-1, model_width),
        got_scaled.reshape(-1, model_width),
        gate_weight,
        up_weight,
        down_weight,
    )
    returned = lax.all_to_all(
        partials.reshape(send_shape), "expert", split_axis=0, concat_axis=0, tiled=True
    )
    returned = returned.reshape(FLIGHT, split_count, HOTCAP, model_width)
    grad_tokens = jnp.einsum(
        "fcr,fpcd->rd", chooser.astype(jnp.bfloat16), returned, preferred_element_type=jnp.float32
    )
    summed = tuple(
        lax.psum_scatter(term, "dp", scatter_dimension=0, tiled=True) for term in grad_terms
    )
    return (grad_tokens.astype(jnp.bfloat16),) + tuple(term.astype(jnp.bfloat16) for term in summed)


HOPS = (7, 4, 2, 1)
CARRIED = len(HOPS) * HOTCAP
NT = (((1,), (1,)), ((), ()))
SMEM = pl.BlockSpec(memory_space=pltpu.SMEM)
VMEM = pl.BlockSpec(memory_space=pltpu.VMEM)
HBM = pl.BlockSpec(memory_space=pltpu.HBM)


def route(hot_experts, routing, gates, modality):
    tok_count, top_count = routing.shape
    hot_count = hot_experts.shape[0]
    slots = FLIGHT * HOTCAP
    hops = len(HOPS)

    def kernel(hot_ref, route_ref, gate_ref, mod_ref, choose_ref, keep_ref, give_ref):
        position = lax.broadcasted_iota(jnp.int32, (top_count, tok_count), 0)
        hot_pick = jnp.zeros((top_count, tok_count), jnp.int32)
        for j in range(hot_count):
            hot_pick = jnp.where(position == top_count - hot_count + j, hot_ref[j], hot_pick)
        pinned = (mod_ref[...] == 1) & (position >= top_count - hot_count)
        chosen = jnp.where(pinned, hot_pick, route_ref[...])
        index = lax.broadcasted_iota(jnp.int32, (FLIGHT, top_count, tok_count), 0)
        hop = jnp.zeros_like(index)
        for k, value in enumerate(HOPS):
            hop = jnp.where(index % hops == k, value, hop)
        expert = hop ^ (index // hops) ^ lax.axis_index("expert") ^ lax.axis_index("dp")
        matches = chosen[None] == expert
        expert_gate = jnp.sum(jnp.where(matches, gate_ref[...][None], 0.0), axis=1)
        present = jnp.sum(jnp.where(matches, 1.0, 0.0), axis=1)
        before = lax.broadcasted_iota(jnp.int32, (tok_count, tok_count), 0)
        after = lax.broadcasted_iota(jnp.int32, (tok_count, tok_count), 1)
        upto = jnp.where(before <= after, 1.0, 0.0).astype(BF16)
        placed = jnp.dot(present.astype(BF16), upto, preferred_element_type=F32)
        slot = lax.broadcasted_iota(jnp.int32, (FLIGHT, HOTCAP, tok_count), 1) + 1
        slot_hit = placed[:, None, :].astype(jnp.int32) == slot
        chooser = slot_hit & (present[:, None, :] > 0.0)
        picker = jnp.where(chooser, 1.0, 0.0).reshape(slots, tok_count)
        gated = jnp.where(chooser, expert_gate[:, None, :], 0.0).reshape(slots, tok_count)
        choose_ref[...] = picker.astype(BF16)
        keep_ref[...] = gated[:CARRIED]
        give_ref[...] = gated[CARRIED:]

    return pl.pallas_call(
        kernel,
        out_shape=[
            pltpu.VMEM((slots, tok_count), BF16),
            pltpu.VMEM((CARRIED, tok_count), F32),
            pltpu.VMEM((slots - CARRIED, tok_count), F32),
        ],
        in_specs=[SMEM, VMEM, VMEM, VMEM],
        out_specs=[VMEM] * 3,
        name="route",
    )(hot_experts, routing.T, gates.T, modality[None, :])


def load_rows(*arrays):
    count = len(arrays)

    def kernel(*refs):
        loads = [
            pltpu.make_async_copy(refs[i], refs[count + i], refs[2 * count].at[i])
            for i in range(count)
        ]
        for load in loads:
            load.start()
        for load in loads:
            load.wait()

    return pl.pallas_call(
        kernel,
        out_shape=[pltpu.VMEM(array.shape, array.dtype) for array in arrays],
        in_specs=[HBM] * count,
        out_specs=[VMEM] * count,
        scratch_shapes=[pltpu.SemaphoreType.DMA((count,))],
        compiler_params=pltpu.CompilerParams(vmem_limit_bytes=2 * MIB),
        cost_estimate=pl.CostEstimate(
            flops=0, bytes_accessed=4 * sum(array.size for array in arrays), transcendentals=0
        ),
        name="load_rows",
    )(*(pltpu.with_memory_space_constraint(array, pltpu.HBM) for array in arrays))


def pick(mine, theirs, my_tokens, their_tokens, my_grads, their_grads):
    tok_count, width = my_tokens.shape

    def kernel(mine_ref, theirs_ref, my_tok, their_tok, my_grad, their_grad, *outs):
        for core, slot_ref, tok_ref, grad_ref in (
            (0, mine_ref, my_tok, my_grad),
            (1, theirs_ref, their_tok, their_grad),
        ):
            gated = slot_ref[...]
            picker = jnp.where(gated != 0.0, 1.0, 0.0).astype(BF16)
            rows = jnp.dot(picker, tok_ref[...], preferred_element_type=F32)
            scaled = jnp.dot(picker, grad_ref[...], preferred_element_type=F32)
            scaled = scaled * jnp.sum(gated, axis=1, keepdims=True)
            for k, out in enumerate(outs):
                slot = slice(k * HOTCAP, (k + 1) * HOTCAP)
                out[core * HOTCAP : (core + 1) * HOTCAP] = rows[slot].astype(BF16)
                out[(core + 2) * HOTCAP : (core + 3) * HOTCAP] = scaled[slot].astype(BF16)

    return pl.pallas_call(
        kernel,
        out_shape=[pltpu.VMEM((4 * HOTCAP, width), BF16)] * len(HOPS),
        in_specs=[VMEM] * 6,
        out_specs=[VMEM] * len(HOPS),
        compiler_params=pltpu.CompilerParams(vmem_limit_bytes=16 * MIB),
        cost_estimate=pl.CostEstimate(
            flops=8 * CARRIED * tok_count * width,
            bytes_accessed=8 * (CARRIED + tok_count) * width,
            transcendentals=0,
        ),
        name="pick",
    )(mine, theirs, my_tokens, their_tokens, my_grads, their_grads)


def load_weights(gate_weight, up_weight, down_weight):
    half = gate_weight.shape[0] // 2
    width = gate_weight.shape[1]
    tile = min(256, half)
    steps = half // tile

    def kernel(g_in, u_in, w_in, g_ref, u_ref, g_cols, u_cols, w_cols, w_ref, sem):
        first = pl.multiple_of(lax.axis_index("dp") * half, half)
        lanes = ((g_in, g_ref, g_cols), (u_in, u_ref, u_cols), (w_in, w_ref, w_cols))
        order = [(lane, i) for lane in range(3) for i in range(steps)]

        def load(lane, i):
            source, target, _ = lanes[lane]
            return pltpu.make_async_copy(
                source.at[pl.ds(first + i * tile, tile)],
                target.at[pl.ds(i * tile, tile)],
                sem.at[lane, i],
            )

        depth = 3
        for step in order[:depth]:
            load(*step).start()
        for n, (lane, i) in enumerate(order):
            load(lane, i).wait()
            if n + depth < len(order):
                load(*order[n + depth]).start()
            _, target, columns = lanes[lane]
            columns[:, i * tile : (i + 1) * tile] = target[i * tile : (i + 1) * tile].T

    return pl.pallas_call(
        kernel,
        out_shape=[pltpu.VMEM((half, width), BF16)] * 2
        + [pltpu.VMEM((width, half), BF16)] * 3,
        in_specs=[HBM] * 3,
        out_specs=[VMEM] * 5,
        scratch_shapes=[pltpu.VMEM((half, width), BF16), pltpu.SemaphoreType.DMA((3, steps))],
        compiler_params=pltpu.CompilerParams(vmem_limit_bytes=10 * MIB),
        cost_estimate=pl.CostEstimate(
            flops=0, bytes_accessed=12 * half * width, transcendentals=0
        ),
        name="load_weights",
    )(
        *(
            pltpu.with_memory_space_constraint(weight, pltpu.HBM)
            for weight in (gate_weight, up_weight, down_weight)
        )
    )


def activation_grads(blocks, gate_half, up_half, gate_cols, up_cols, down_cols):
    width = blocks[0].shape[1]
    rows = 2 * HOTCAP * len(HOPS)
    half = gate_half.shape[0]
    tile = min(512, half)
    chunk = 512 if width % 512 == 0 else width

    def kernel(*refs):
        ins, refs = refs[: len(blocks)], refs[len(blocks) :]
        g_ref, u_ref, g_cols, u_cols, w_cols, tok_ref, scl_ref = refs[:7]
        dh_ref, du_ref, act_ref, mine_ref, theirs_ref, dh_rows, du_rows = refs[7:]
        message = 2 * HOTCAP
        place = 0
        for block in ins:
            for start in range(0, block.shape[0], 2 * message):
                tok_ref[place : place + message] = block[start : start + message]
                scl_ref[place : place + message] = block[start + message : start + 2 * message]
                place += message
        for i in range(half // tile):
            part = slice(i * tile, (i + 1) * tile)
            pre = jnp.dot(tok_ref[...], g_cols[:, part], preferred_element_type=F32)
            up = jnp.dot(tok_ref[...], u_cols[:, part], preferred_element_type=F32)
            da = jnp.dot(scl_ref[...], w_cols[:, part], preferred_element_type=F32)
            sig = jax.nn.sigmoid(pre)
            swish = pre * sig
            act_ref[part] = (swish * up).astype(BF16).T
            dh = (da * up * sig * (1.0 + pre * (1.0 - sig))).astype(BF16)
            du = (da * swish).astype(BF16)
            dh_ref[part] = dh.T
            du_ref[part] = du.T
            dh_rows[:, part] = dh
            du_rows[:, part] = du
        for c in range(0, width, chunk):
            cols = slice(c, c + chunk)
            piece = jnp.dot(dh_rows[...], g_ref[:, cols], preferred_element_type=F32)
            piece += jnp.dot(du_rows[...], u_ref[:, cols], preferred_element_type=F32)
            mine_ref[:, cols] = piece[:rows]
            theirs_ref[:, cols] = piece[rows:].astype(BF16)

    return pl.pallas_call(
        kernel,
        out_shape=[pltpu.VMEM((2 * rows, width), BF16)] * 2
        + [pltpu.VMEM((half, 2 * rows), BF16)] * 3
        + [pltpu.VMEM((rows, width), F32), pltpu.VMEM((rows, width), BF16)],
        in_specs=[VMEM] * (len(blocks) + 5),
        out_specs=[VMEM] * 7,
        scratch_shapes=[pltpu.VMEM((2 * rows, half), BF16)] * 2,
        compiler_params=pltpu.CompilerParams(vmem_limit_bytes=8 * MIB),
        cost_estimate=pl.CostEstimate(
            flops=20 * rows * half * width,
            bytes_accessed=6 * half * width,
            transcendentals=2 * rows * half,
        ),
        name="activation_grads",
    )(*blocks, gate_half, up_half, gate_cols, up_cols, down_cols)


def column_chunks(width):
    chunk = 512 if width % 512 == 0 else width
    return [slice(c, c + chunk) for c in range(0, width, chunk)]


def written_after(chunks):
    return 2 * len(chunks) // 7, 5 * len(chunks) // 7


def down_grads(rows, left):
    count, width = rows.shape
    half = left.shape[0]
    chunks = column_chunks(width)
    early = len(chunks) // 2

    def kernel(rows_ref, left_ref, held, out, sem):
        copies = []
        for n, cols in enumerate(chunks):
            held[:, cols] = jnp.dot(
                left_ref[...], rows_ref[:, cols], preferred_element_type=F32
            ).astype(BF16)
            if n < early:
                copies.append(
                    pltpu.make_async_copy(held.at[:, cols], out.at[:, cols], sem.at[n])
                )
                copies[-1].start()
        for copy in copies:
            copy.wait()

    return pl.pallas_call(
        kernel,
        out_shape=[
            pltpu.VMEM((half, width), BF16),
            jax.ShapeDtypeStruct((half, width), BF16),
        ],
        in_specs=[VMEM, VMEM],
        out_specs=[VMEM, HBM],
        scratch_shapes=[pltpu.SemaphoreType.DMA((len(chunks),))],
        compiler_params=pltpu.CompilerParams(vmem_limit_bytes=8 * MIB),
        cost_estimate=pl.CostEstimate(
            flops=2 * count * half * width, bytes_accessed=2 * half * width, transcendentals=0
        ),
        name="down_grads",
    )(rows, left)


def gate_up_grads(rows, gate_left, up_left, down, down_written):
    count, width = rows.shape
    half = gate_left.shape[0]
    chunks = column_chunks(width)
    early = len(chunks) // 2
    shares = written_after(chunks)

    def kernel(rows_ref, gate_ref, up_ref, down_ref, _, *refs):
        gate_out, down_out, up_held, up_out, held, sem = refs
        copies = []
        for n, cols in enumerate(chunks):
            if n >= early:
                copies.append(
                    pltpu.make_async_copy(down_ref.at[:, cols], down_out.at[:, cols], sem.at[0, n])
                )
                copies[-1].start()
        for n, cols in enumerate(chunks):
            held[:, cols] = jnp.dot(
                gate_ref[...], rows_ref[:, cols], preferred_element_type=F32
            ).astype(BF16)
            copies.append(
                pltpu.make_async_copy(held.at[:, cols], gate_out.at[:, cols], sem.at[1, n])
            )
            copies[-1].start()
        for n, cols in enumerate(chunks):
            up_held[:, cols] = jnp.dot(
                up_ref[...], rows_ref[:, cols], preferred_element_type=F32
            ).astype(BF16)
            if n < shares[0]:
                copies.append(
                    pltpu.make_async_copy(up_held.at[:, cols], up_out.at[:, cols], sem.at[2, n])
                )
                copies[-1].start()
        for copy in copies:
            copy.wait()

    full = jax.ShapeDtypeStruct((half, width), BF16)
    return pl.pallas_call(
        kernel,
        out_shape=[full, full, pltpu.VMEM((half, width), BF16), full],
        in_specs=[VMEM] * 4 + [HBM],
        out_specs=[HBM, HBM, VMEM, HBM],
        scratch_shapes=[
            pltpu.VMEM((half, width), BF16),
            pltpu.SemaphoreType.DMA((3, len(chunks))),
        ],
        input_output_aliases={4: 1},
        compiler_params=pltpu.CompilerParams(vmem_limit_bytes=12 * MIB),
        cost_estimate=pl.CostEstimate(
            flops=4 * count * half * width, bytes_accessed=4 * half * width, transcendentals=0
        ),
        name="gate_up_grads",
    )(rows, gate_left, up_left, down, down_written)


def write_more(block, written):
    chunks = column_chunks(block.shape[1])
    start, stop = written_after(chunks)
    first = chunks[start].start
    cols = pl.ds(first, chunks[stop].start - first)

    def kernel(block_ref, _, out, sem):
        copy = pltpu.make_async_copy(block_ref.at[:, cols], out.at[:, cols], sem)
        copy.start()
        copy.wait()

    return pl.pallas_call(
        kernel,
        out_shape=jax.ShapeDtypeStruct(block.shape, block.dtype),
        in_specs=[VMEM, HBM],
        out_specs=HBM,
        scratch_shapes=[pltpu.SemaphoreType.DMA],
        input_output_aliases={1: 0},
        compiler_params=pltpu.CompilerParams(vmem_limit_bytes=2 * MIB),
        cost_estimate=pl.CostEstimate(
            flops=0, bytes_accessed=2 * block.size, transcendentals=0
        ),
        name="write_more",
    )(block, written)


def combine(picker, returned, block, written):
    slots, tok_count = picker.shape
    width = returned.shape[1]
    chunks = column_chunks(width)
    first = chunks[written_after(chunks)[1]].start

    def kernel(pick_ref, back_ref, block_ref, _, sum_out, block_out, held, sem):
        rest = pl.ds(first, width - first)
        copies = [pltpu.make_async_copy(block_ref.at[:, rest], block_out.at[:, rest], sem.at[0])]
        copies[0].start()
        chooser = pick_ref[...].T
        for n, cols in enumerate(chunks):
            held[:, cols] = jnp.dot(
                chooser, back_ref[:, cols], preferred_element_type=F32
            ).astype(BF16)
            copies.append(
                pltpu.make_async_copy(held.at[:, cols], sum_out.at[:, cols], sem.at[1 + n])
            )
            copies[-1].start()
        for copy in copies:
            copy.wait()

    return pl.pallas_call(
        kernel,
        out_shape=[
            jax.ShapeDtypeStruct((tok_count, width), BF16),
            jax.ShapeDtypeStruct(block.shape, block.dtype),
        ],
        in_specs=[VMEM, VMEM, VMEM, HBM],
        out_specs=[HBM, HBM],
        scratch_shapes=[
            pltpu.VMEM((tok_count, width), BF16),
            pltpu.SemaphoreType.DMA((1 + len(chunks),)),
        ],
        input_output_aliases={3: 1},
        compiler_params=pltpu.CompilerParams(vmem_limit_bytes=4 * MIB),
        cost_estimate=pl.CostEstimate(
            flops=2 * slots * tok_count * width,
            bytes_accessed=2 * tok_count * width + block.size,
            transcendentals=0,
        ),
        name="combine",
    )(picker, returned, block, written)


def per_device(
    tokens, grad_out, routing, gates, modality, hot_experts, gate_weight, up_weight, down_weight
):
    def swap(block):
        return lax.ppermute(block, "dp", [(0, 1), (1, 0)])

    def travel(block, hop):
        moves = [
            (2 * i + c, 2 * (i ^ hop ^ c) + c) for i in range(FLIGHT) for c in range(2)
        ]
        return lax.ppermute(block, ("expert", "dp"), moves)

    picker, keep, give = route(hot_experts, routing, gates, modality)
    my_tokens, my_grads = load_rows(tokens, grad_out)
    msgs = pick(keep, swap(give), my_tokens, swap(tokens), my_grads, swap(grad_out))
    got = [travel(m, hop) for m, hop in zip(msgs, HOPS)]
    halves = load_weights(gate_weight, up_weight, down_weight)
    got, halves = lax.optimization_barrier((got, halves))
    own = jnp.concatenate(got, axis=0)
    blocks = [own, swap(own)]
    tok, scl, dh, du, act, mine, theirs = activation_grads(blocks, *halves)
    down = down_grads(scl, act)
    added, down = lax.optimization_barrier((swap(theirs), down))
    pieces = (mine + added.astype(F32)).astype(BF16)
    back = [
        travel(pieces[2 * k * HOTCAP : 2 * (k + 1) * HOTCAP], hop) for k, hop in enumerate(HOPS)
    ]
    grad_gate, grad_down, up_block, written = gate_up_grads(tok, dh, du, *down)
    back, up_block = lax.optimization_barrier((back[::-1], up_block))
    back = back[::-1]
    kept = jnp.concatenate([block[:HOTCAP] for block in back], axis=0)
    given = swap(jnp.concatenate([block[HOTCAP:] for block in back], axis=0))
    given, written = lax.optimization_barrier((given, write_more(up_block, written)))
    returned = jnp.concatenate([kept, given], axis=0)
    grad_tokens, grad_up = combine(picker, returned, up_block, written)
    return grad_tokens, grad_gate, grad_up, grad_down


def solution(mesh):
    sizes = dict(mesh.shape)
    token_spec = P(("groups", "expert", "dp"), None)
    in_specs = (
        token_spec,
        token_spec,
        token_spec,
        token_spec,
        P(("groups", "expert", "dp")),
        P("groups"),
        P("expert", None),
        P("expert", None),
        P("expert", None),
    )
    paired = sizes["expert"] == FLIGHT and sizes["dp"] == 2
    return jax.shard_map(
        per_device if paired else per_device_general,
        mesh=mesh,
        in_specs=in_specs,
        out_specs=(token_spec,) * 4,
        check_vma=False,
    )
```

```python
import jax
import jax.numpy as jnp
from jax import lax
from jax.experimental import pallas as pl
from jax.experimental.pallas import tpu as pltpu
from jax.sharding import PartitionSpec as P

FLIGHT = 8
HOTCAP = 8
F32 = jnp.float32
BF16 = jnp.bfloat16
MIB = 1 << 20


def expert_pass(in_tokens, in_scaled, gate_rows, up_rows, down_rows):
    pre_gate = jnp.einsum("nd,hd->nh", in_tokens, gate_rows, preferred_element_type=jnp.float32)
    pre_up = jnp.einsum("nd,hd->nh", in_tokens, up_rows, preferred_element_type=jnp.float32)
    sigmoid_gate = jax.nn.sigmoid(pre_gate)
    swish_gate = pre_gate * sigmoid_gate
    activated = (swish_gate * pre_up).astype(jnp.bfloat16)
    grad_act = jnp.einsum("nd,hd->nh", in_scaled, down_rows, preferred_element_type=jnp.float32)
    grad_pre_gate = (
        grad_act * pre_up * sigmoid_gate * (1.0 + pre_gate * (1.0 - sigmoid_gate))
    ).astype(jnp.bfloat16)
    grad_pre_up = (grad_act * swish_gate).astype(jnp.bfloat16)
    gate_term = jnp.einsum(
        "nh,nd->hd", grad_pre_gate, in_tokens, preferred_element_type=jnp.float32
    )
    up_term = jnp.einsum("nh,nd->hd", grad_pre_up, in_tokens, preferred_element_type=jnp.float32)
    down_term = jnp.einsum("nh,nd->hd", activated, in_scaled, preferred_element_type=jnp.float32)
    partials = jnp.dot(grad_pre_gate, gate_rows, preferred_element_type=jnp.float32)
    partials = (
        partials + jnp.dot(grad_pre_up, up_rows, preferred_element_type=jnp.float32)
    ).astype(jnp.bfloat16)
    return (partials, (gate_term, up_term, down_term))


def per_device_general(
    tokens, grad_out, routing, gates, modality, hot_experts, gate_weight, up_weight, down_weight
):
    tok_count, model_width = tokens.shape
    top_count = routing.shape[1]
    hot_count = hot_experts.shape[0]
    devices = lax.axis_size("expert")
    split_count = devices // FLIGHT
    position = lax.broadcasted_iota(jnp.int32, (tok_count, top_count), 1)
    pinned_slot = position - (top_count - hot_count)
    pick_table = pinned_slot[:, :, None] == jnp.arange(hot_count, dtype=jnp.int32)[None, None, :]
    hot_pick = jnp.sum(jnp.where(pick_table, hot_experts[None, None, :], 0), axis=2)
    pinned = (modality[:, None] == 1) & (pinned_slot >= 0)
    chosen = jnp.where(pinned, hot_pick, routing)
    matches = chosen[:, :, None] == jnp.arange(FLIGHT, dtype=jnp.int32)[None, None, :]
    expert_gate = jnp.sum(jnp.where(matches, gates[:, :, None], 0.0), axis=1)
    present = jnp.any(matches, axis=1)
    placed = jnp.cumsum(present.astype(jnp.int32), axis=0) - 1
    slot_ids = jnp.arange(HOTCAP, dtype=jnp.int32)
    chooser = (placed.T[:, None, :] == slot_ids[None, :, None]) & present.T[:, None, :]
    picker = chooser.astype(jnp.bfloat16)
    picked = jnp.einsum("scr,rd->scd", picker, tokens, preferred_element_type=jnp.float32).astype(
        jnp.bfloat16
    )
    picked_grad = jnp.einsum("scr,rd->scd", picker, grad_out, preferred_element_type=jnp.float32)
    slot_gate = jnp.sum(jnp.where(chooser, expert_gate.T[:, None, :], 0.0), axis=2)
    scaled = (picked_grad * slot_gate[:, :, None]).astype(jnp.bfloat16)
    send_shape = (devices, HOTCAP, model_width)

    def replicate_rows(block_data):
        widened = jnp.broadcast_to(block_data[:, None], (FLIGHT, split_count, HOTCAP, model_width))
        return widened.reshape(send_shape)

    got_tokens, got_scaled = (
        lax.all_to_all(replicate_rows(picked), "expert", split_axis=0, concat_axis=0, tiled=True),
        lax.all_to_all(replicate_rows(scaled), "expert", split_axis=0, concat_axis=0, tiled=True),
    )
    partials, grad_terms = expert_pass(
        got_tokens.reshape(-1, model_width),
        got_scaled.reshape(-1, model_width),
        gate_weight,
        up_weight,
        down_weight,
    )
    returned = lax.all_to_all(
        partials.reshape(send_shape), "expert", split_axis=0, concat_axis=0, tiled=True
    )
    returned = returned.reshape(FLIGHT, split_count, HOTCAP, model_width)
    grad_tokens = jnp.einsum(
        "fcr,fpcd->rd", chooser.astype(jnp.bfloat16), returned, preferred_element_type=jnp.float32
    )
    summed = tuple(
        lax.psum_scatter(term, "dp", scatter_dimension=0, tiled=True) for term in grad_terms
    )
    return (grad_tokens.astype(jnp.bfloat16),) + tuple(term.astype(jnp.bfloat16) for term in summed)


HOPS = (7, 4, 2, 1)
CARRIED = len(HOPS) * HOTCAP
NT = (((1,), (1,)), ((), ()))
SMEM = pl.BlockSpec(memory_space=pltpu.SMEM)
VMEM = pl.BlockSpec(memory_space=pltpu.VMEM)
HBM = pl.BlockSpec(memory_space=pltpu.HBM)


def route(hot_experts, routing, gates, modality):
    tok_count, top_count = routing.shape
    hot_count = hot_experts.shape[0]
    slots = FLIGHT * HOTCAP
    hops = len(HOPS)

    def kernel(hot_ref, route_ref, gate_ref, mod_ref, choose_ref, keep_ref, give_ref):
        position = lax.broadcasted_iota(jnp.int32, (top_count, tok_count), 0)
        hot_pick = jnp.zeros((top_count, tok_count), jnp.int32)
        for j in range(hot_count):
            hot_pick = jnp.where(position == top_count - hot_count + j, hot_ref[j], hot_pick)
        pinned = (mod_ref[...] == 1) & (position >= top_count - hot_count)
        chosen = jnp.where(pinned, hot_pick, route_ref[...])
        index = lax.broadcasted_iota(jnp.int32, (FLIGHT, top_count, tok_count), 0)
        hop = jnp.zeros_like(index)
        for k, value in enumerate(HOPS):
            hop = jnp.where(index % hops == k, value, hop)
        expert = hop ^ (index // hops) ^ lax.axis_index("expert") ^ lax.axis_index("dp")
        matches = chosen[None] == expert
        expert_gate = jnp.sum(jnp.where(matches, gate_ref[...][None], 0.0), axis=1)
        present = jnp.sum(jnp.where(matches, 1.0, 0.0), axis=1)
        before = lax.broadcasted_iota(jnp.int32, (tok_count, tok_count), 0)
        after = lax.broadcasted_iota(jnp.int32, (tok_count, tok_count), 1)
        upto = jnp.where(before <= after, 1.0, 0.0).astype(BF16)
        placed = jnp.dot(present.astype(BF16), upto, preferred_element_type=F32)
        slot = lax.broadcasted_iota(jnp.int32, (FLIGHT, HOTCAP, tok_count), 1) + 1
        slot_hit = placed[:, None, :].astype(jnp.int32) == slot
        chooser = slot_hit & (present[:, None, :] > 0.0)
        picker = jnp.where(chooser, 1.0, 0.0).reshape(slots, tok_count)
        gated = jnp.where(chooser, expert_gate[:, None, :], 0.0).reshape(slots, tok_count)
        choose_ref[...] = picker.astype(BF16)
        keep_ref[...] = gated[:CARRIED]
        give_ref[...] = gated[CARRIED:]

    return pl.pallas_call(
        kernel,
        out_shape=[
            pltpu.VMEM((slots, tok_count), BF16),
            pltpu.VMEM((CARRIED, tok_count), F32),
            pltpu.VMEM((slots - CARRIED, tok_count), F32),
        ],
        in_specs=[SMEM, VMEM, VMEM, VMEM],
        out_specs=[VMEM] * 3,
        name="route",
    )(hot_experts, routing.T, gates.T, modality[None, :])


def load_rows(*arrays):
    count = len(arrays)

    def kernel(*refs):
        loads = [
            pltpu.make_async_copy(refs[i], refs[count + i], refs[2 * count].at[i])
            for i in range(count)
        ]
        for load in loads:
            load.start()
        for load in loads:
            load.wait()

    return pl.pallas_call(
        kernel,
        out_shape=[pltpu.VMEM(array.shape, array.dtype) for array in arrays],
        in_specs=[HBM] * count,
        out_specs=[VMEM] * count,
        scratch_shapes=[pltpu.SemaphoreType.DMA((count,))],
        compiler_params=pltpu.CompilerParams(vmem_limit_bytes=2 * MIB),
        cost_estimate=pl.CostEstimate(
            flops=0, bytes_accessed=4 * sum(array.size for array in arrays), transcendentals=0
        ),
        name="load_rows",
    )(*(pltpu.with_memory_space_constraint(array, pltpu.HBM) for array in arrays))


def pick(mine, theirs, my_tokens, their_tokens, my_grads, their_grads):
    tok_count, width = my_tokens.shape

    def kernel(mine_ref, theirs_ref, my_tok, their_tok, my_grad, their_grad, *outs):
        for core, slot_ref, tok_ref, grad_ref in (
            (0, mine_ref, my_tok, my_grad),
            (1, theirs_ref, their_tok, their_grad),
        ):
            gated = slot_ref[...]
            picker = jnp.where(gated != 0.0, 1.0, 0.0).astype(BF16)
            rows = jnp.dot(picker, tok_ref[...], preferred_element_type=F32)
            scaled = jnp.dot(picker, grad_ref[...], preferred_element_type=F32)
            scaled = scaled * jnp.sum(gated, axis=1, keepdims=True)
            for k, out in enumerate(outs):
                slot = slice(k * HOTCAP, (k + 1) * HOTCAP)
                out[core * HOTCAP : (core + 1) * HOTCAP] = rows[slot].astype(BF16)
                out[(core + 2) * HOTCAP : (core + 3) * HOTCAP] = scaled[slot].astype(BF16)

    return pl.pallas_call(
        kernel,
        out_shape=[pltpu.VMEM((4 * HOTCAP, width), BF16)] * len(HOPS),
        in_specs=[VMEM] * 6,
        out_specs=[VMEM] * len(HOPS),
        compiler_params=pltpu.CompilerParams(vmem_limit_bytes=16 * MIB),
        cost_estimate=pl.CostEstimate(
            flops=8 * CARRIED * tok_count * width,
            bytes_accessed=8 * (CARRIED + tok_count) * width,
            transcendentals=0,
        ),
        name="pick",
    )(mine, theirs, my_tokens, their_tokens, my_grads, their_grads)


def load_weights(gate_weight, up_weight, down_weight):
    half = gate_weight.shape[0] // 2
    width = gate_weight.shape[1]
    tile = min(256, half)
    steps = half // tile

    def kernel(g_in, u_in, w_in, g_ref, u_ref, g_cols, u_cols, w_cols, w_ref, sem):
        first = pl.multiple_of(lax.axis_index("dp") * half, half)
        lanes = ((g_in, g_ref, g_cols), (u_in, u_ref, u_cols), (w_in, w_ref, w_cols))
        order = [(lane, i) for lane in range(3) for i in range(steps)]

        def load(lane, i):
            source, target, _ = lanes[lane]
            return pltpu.make_async_copy(
                source.at[pl.ds(first + i * tile, tile)],
                target.at[pl.ds(i * tile, tile)],
                sem.at[lane, i],
            )

        depth = 3
        for step in order[:depth]:
            load(*step).start()
        for n, (lane, i) in enumerate(order):
            load(lane, i).wait()
            if n + depth < len(order):
                load(*order[n + depth]).start()
            _, target, columns = lanes[lane]
            columns[:, i * tile : (i + 1) * tile] = target[i * tile : (i + 1) * tile].T

    return pl.pallas_call(
        kernel,
        out_shape=[pltpu.VMEM((half, width), BF16)] * 2
        + [pltpu.VMEM((width, half), BF16)] * 3,
        in_specs=[HBM] * 3,
        out_specs=[VMEM] * 5,
        scratch_shapes=[pltpu.VMEM((half, width), BF16), pltpu.SemaphoreType.DMA((3, steps))],
        compiler_params=pltpu.CompilerParams(vmem_limit_bytes=10 * MIB),
        cost_estimate=pl.CostEstimate(
            flops=0, bytes_accessed=12 * half * width, transcendentals=0
        ),
        name="load_weights",
    )(
        *(
            pltpu.with_memory_space_constraint(weight, pltpu.HBM)
            for weight in (gate_weight, up_weight, down_weight)
        )
    )


def activation_grads(blocks, gate_half, up_half, gate_cols, up_cols, down_cols):
    width = blocks[0].shape[1]
    rows = 2 * HOTCAP * len(HOPS)
    half = gate_half.shape[0]
    tile = min(512, half)
    chunk = 512 if width % 512 == 0 else width

    def kernel(*refs):
        ins, refs = refs[: len(blocks)], refs[len(blocks) :]
        g_ref, u_ref, g_cols, u_cols, w_cols, tok_ref, scl_ref = refs[:7]
        dh_ref, du_ref, act_ref, mine_ref, theirs_ref, dh_rows, du_rows = refs[7:]
        message = 2 * HOTCAP
        place = 0
        for block in ins:
            for start in range(0, block.shape[0], 2 * message):
                tok_ref[place : place + message] = block[start : start + message]
                scl_ref[place : place + message] = block[start + message : start + 2 * message]
                place += message
        for i in range(half // tile):
            part = slice(i * tile, (i + 1) * tile)
            pre = jnp.dot(tok_ref[...], g_cols[:, part], preferred_element_type=F32)
            up = jnp.dot(tok_ref[...], u_cols[:, part], preferred_element_type=F32)
            da = jnp.dot(scl_ref[...], w_cols[:, part], preferred_element_type=F32)
            sig = jax.nn.sigmoid(pre)
            swish = pre * sig
            act_ref[part] = (swish * up).astype(BF16).T
            dh = (da * up * sig * (1.0 + pre * (1.0 - sig))).astype(BF16)
            du = (da * swish).astype(BF16)
            dh_ref[part] = dh.T
            du_ref[part] = du.T
            dh_rows[:, part] = dh
            du_rows[:, part] = du
        for c in range(0, width, chunk):
            cols = slice(c, c + chunk)
            piece = jnp.dot(dh_rows[...], g_ref[:, cols], preferred_element_type=F32)
            piece += jnp.dot(du_rows[...], u_ref[:, cols], preferred_element_type=F32)
            mine_ref[:, cols] = piece[:rows]
            theirs_ref[:, cols] = piece[rows:].astype(BF16)

    return pl.pallas_call(
        kernel,
        out_shape=[pltpu.VMEM((2 * rows, width), BF16)] * 2
        + [pltpu.VMEM((half, 2 * rows), BF16)] * 3
        + [pltpu.VMEM((rows, width), F32), pltpu.VMEM((rows, width), BF16)],
        in_specs=[VMEM] * (len(blocks) + 5),
        out_specs=[VMEM] * 7,
        scratch_shapes=[pltpu.VMEM((2 * rows, half), BF16)] * 2,
        compiler_params=pltpu.CompilerParams(vmem_limit_bytes=8 * MIB),
        cost_estimate=pl.CostEstimate(
            flops=20 * rows * half * width,
            bytes_accessed=6 * half * width,
            transcendentals=2 * rows * half,
        ),
        name="activation_grads",
    )(*blocks, gate_half, up_half, gate_cols, up_cols, down_cols)


def column_chunks(width):
    chunk = 512 if width % 512 == 0 else width
    return [slice(c, c + chunk) for c in range(0, width, chunk)]


def written_after(chunks):
    return 2 * len(chunks) // 7, 5 * len(chunks) // 7


def down_grads(rows, left):
    count, width = rows.shape
    half = left.shape[0]
    chunks = column_chunks(width)
    early = len(chunks) // 2

    def kernel(rows_ref, left_ref, held, out, sem):
        copies = []
        for n, cols in enumerate(chunks):
            held[:, cols] = jnp.dot(
                left_ref[...], rows_ref[:, cols], preferred_element_type=F32
            ).astype(BF16)
            if n < early:
                copies.append(
                    pltpu.make_async_copy(held.at[:, cols], out.at[:, cols], sem.at[n])
                )
                copies[-1].start()
        for copy in copies:
            copy.wait()

    return pl.pallas_call(
        kernel,
        out_shape=[
            pltpu.VMEM((half, width), BF16),
            jax.ShapeDtypeStruct((half, width), BF16),
        ],
        in_specs=[VMEM, VMEM],
        out_specs=[VMEM, HBM],
        scratch_shapes=[pltpu.SemaphoreType.DMA((len(chunks),))],
        compiler_params=pltpu.CompilerParams(vmem_limit_bytes=8 * MIB),
        cost_estimate=pl.CostEstimate(
            flops=2 * count * half * width, bytes_accessed=2 * half * width, transcendentals=0
        ),
        name="down_grads",
    )(rows, left)


def gate_up_grads(rows, gate_left, up_left, down, down_written):
    count, width = rows.shape
    half = gate_left.shape[0]
    chunks = column_chunks(width)
    early = len(chunks) // 2
    shares = written_after(chunks)

    def kernel(rows_ref, gate_ref, up_ref, down_ref, _, *refs):
        gate_out, down_out, up_held, up_out, held, sem = refs
        copies = []
        for n, cols in enumerate(chunks):
            if n >= early:
                copies.append(
                    pltpu.make_async_copy(down_ref.at[:, cols], down_out.at[:, cols], sem.at[0, n])
                )
                copies[-1].start()
        for n, cols in enumerate(chunks):
            held[:, cols] = jnp.dot(
                gate_ref[...], rows_ref[:, cols], preferred_element_type=F32
            ).astype(BF16)
            copies.append(
                pltpu.make_async_copy(held.at[:, cols], gate_out.at[:, cols], sem.at[1, n])
            )
            copies[-1].start()
        for n, cols in enumerate(chunks):
            up_held[:, cols] = jnp.dot(
                up_ref[...], rows_ref[:, cols], preferred_element_type=F32
            ).astype(BF16)
            if n < shares[0]:
                copies.append(
                    pltpu.make_async_copy(up_held.at[:, cols], up_out.at[:, cols], sem.at[2, n])
                )
                copies[-1].start()
        for copy in copies:
            copy.wait()

    full = jax.ShapeDtypeStruct((half, width), BF16)
    return pl.pallas_call(
        kernel,
        out_shape=[full, full, pltpu.VMEM((half, width), BF16), full],
        in_specs=[VMEM] * 4 + [HBM],
        out_specs=[HBM, HBM, VMEM, HBM],
        scratch_shapes=[
            pltpu.VMEM((half, width), BF16),
            pltpu.SemaphoreType.DMA((3, len(chunks))),
        ],
        input_output_aliases={4: 1},
        compiler_params=pltpu.CompilerParams(vmem_limit_bytes=12 * MIB),
        cost_estimate=pl.CostEstimate(
            flops=4 * count * half * width, bytes_accessed=4 * half * width, transcendentals=0
        ),
        name="gate_up_grads",
    )(rows, gate_left, up_left, down, down_written)


def write_more(block, written):
    chunks = column_chunks(block.shape[1])
    start, stop = written_after(chunks)
    first = chunks[start].start
    cols = pl.ds(first, chunks[stop].start - first)

    def kernel(block_ref, _, out, sem):
        copy = pltpu.make_async_copy(block_ref.at[:, cols], out.at[:, cols], sem)
        copy.start()
        copy.wait()

    return pl.pallas_call(
        kernel,
        out_shape=jax.ShapeDtypeStruct(block.shape, block.dtype),
        in_specs=[VMEM, HBM],
        out_specs=HBM,
        scratch_shapes=[pltpu.SemaphoreType.DMA],
        input_output_aliases={1: 0},
        compiler_params=pltpu.CompilerParams(vmem_limit_bytes=2 * MIB),
        cost_estimate=pl.CostEstimate(
            flops=0, bytes_accessed=2 * block.size, transcendentals=0
        ),
        name="write_more",
    )(block, written)


def combine(picker, returned, block, written):
    slots, tok_count = picker.shape
    width = returned.shape[1]
    chunks = column_chunks(width)
    first = chunks[written_after(chunks)[1]].start

    def kernel(pick_ref, back_ref, block_ref, _, sum_out, block_out, held, sem):
        rest = pl.ds(first, width - first)
        copies = [pltpu.make_async_copy(block_ref.at[:, rest], block_out.at[:, rest], sem.at[0])]
        copies[0].start()
        chooser = pick_ref[...].T
        for n, cols in enumerate(chunks):
            held[:, cols] = jnp.dot(
                chooser, back_ref[:, cols], preferred_element_type=F32
            ).astype(BF16)
            copies.append(
                pltpu.make_async_copy(held.at[:, cols], sum_out.at[:, cols], sem.at[1 + n])
            )
            copies[-1].start()
        for copy in copies:
            copy.wait()

    return pl.pallas_call(
        kernel,
        out_shape=[
            jax.ShapeDtypeStruct((tok_count, width), BF16),
            jax.ShapeDtypeStruct(block.shape, block.dtype),
        ],
        in_specs=[VMEM, VMEM, VMEM, HBM],
        out_specs=[HBM, HBM],
        scratch_shapes=[
            pltpu.VMEM((tok_count, width), BF16),
            pltpu.SemaphoreType.DMA((1 + len(chunks),)),
        ],
        input_output_aliases={3: 1},
        compiler_params=pltpu.CompilerParams(vmem_limit_bytes=4 * MIB),
        cost_estimate=pl.CostEstimate(
            flops=2 * slots * tok_count * width,
            bytes_accessed=2 * tok_count * width + block.size,
            transcendentals=0,
        ),
        name="combine",
    )(picker, returned, block, written)


def per_device(
    tokens, grad_out, routing, gates, modality, hot_experts, gate_weight, up_weight, down_weight
):
    def swap(block):
        return lax.ppermute(block, "dp", [(0, 1), (1, 0)])

    def travel(block, hop, cross=0):
        moves = [
            (2 * i + c, 2 * (i ^ hop ^ c) + (c ^ cross)) for i in range(FLIGHT) for c in range(2)
        ]
        return lax.ppermute(block, ("expert", "dp"), moves)

    picker, keep, give = route(hot_experts, routing, gates, modality)
    my_tokens, my_grads = load_rows(tokens, grad_out)
    msgs = pick(keep, swap(give), my_tokens, swap(tokens), my_grads, swap(grad_out))
    got = [travel(m, hop) for m, hop in zip(msgs, HOPS)]
    halves = load_weights(gate_weight, up_weight, down_weight)
    nearest = travel(msgs[-1], HOPS[-1], 1)
    got, nearest, halves = lax.optimization_barrier((got, nearest, halves))
    far = jnp.concatenate(got[:-1], axis=0)
    blocks = [far, got[-1], swap(far), nearest]
    tok, scl, dh, du, act, mine, theirs = activation_grads(blocks, *halves)
    down = down_grads(scl, act)
    added, down = lax.optimization_barrier((swap(theirs), down))
    pieces = (mine + added.astype(F32)).astype(BF16)
    back = [
        travel(pieces[2 * k * HOTCAP : 2 * (k + 1) * HOTCAP], hop) for k, hop in enumerate(HOPS)
    ]
    grad_gate, grad_down, up_block, written = gate_up_grads(tok, dh, du, *down)
    back, up_block = lax.optimization_barrier((back[::-1], up_block))
    back = back[::-1]
    kept = jnp.concatenate([block[:HOTCAP] for block in back], axis=0)
    given = swap(jnp.concatenate([block[HOTCAP:] for block in back], axis=0))
    given, written = lax.optimization_barrier((given, write_more(up_block, written)))
    returned = jnp.concatenate([kept, given], axis=0)
    grad_tokens, grad_up = combine(picker, returned, up_block, written)
    return grad_tokens, grad_gate, grad_up, grad_down


def solution(mesh):
    sizes = dict(mesh.shape)
    token_spec = P(("groups", "expert", "dp"), None)
    in_specs = (
        token_spec,
        token_spec,
        token_spec,
        token_spec,
        P(("groups", "expert", "dp")),
        P("groups"),
        P("expert", None),
        P("expert", None),
        P("expert", None),
    )
    paired = sizes["expert"] == FLIGHT and sizes["dp"] == 2
    return jax.shard_map(
        per_device if paired else per_device_general,
        mesh=mesh,
        in_specs=in_specs,
        out_specs=(token_spec,) * 4,
        check_vma=False,
    )
```
